32 devices in a mesh: rep: 2 (over y), head: 4 (over x, core), row: 4 (over z).
Axes of the slice: x: 2, y: 2, z: 4, core: 2. Of those that a mesh axis runs over, the one named last changes fastest.
Arguments:
- hidden: bfloat16 [256, 2, 8192], P(('rep', 'row'), None, 'head'), parts along dimension 0, may hold values from -6 to 6
- input_norm_scale: float32 [8192], P('head'), may hold values from 0.5 to 1.5
- projection_signal: bfloat16 [8192, 4096], P('row', 'head'), may hold values from -0.0625 to 0.0625
- projection_gate: bfloat16 [8192, 4096], P('row', 'head'), may hold values from -0.0625 to 0.0625
- projection_step: bfloat16 [8192, 64], P('row', 'head'), may hold values from -0.0625 to 0.0625
- projection_input_output: bfloat16 [8192, 256], P('row'), may hold values from -0.0625 to 0.0625
- step_bias: float32 [64], P('head'), may hold values from -4 to 0
- head_decay_rate: float32 [64], P('head'), may hold values from 0.5 to 16
- head_skip_weight: float32 [64], P('head'), may hold values from 0.5 to 1.5
- gated_norm_scale: float32 [4096], P('head'), may hold values from 0.5 to 1.5
- adapter_down_weight: bfloat16 [512, 8192, 16], P('row', 'head'), may hold values from -0.0625 to 0.0625
- adapter_up_weight: bfloat16 [512, 16, 4096], P('row', None, 'head'), may hold values from -1.5 to 1.5
- output_weight: bfloat16 [4096, 8192], P('head'), may hold values from -0.125 to 0.125
- scan_state: bfloat16 [256, 64, 64, 128], P(('rep', 'row'), 'head'), parts along dimension 0, may hold values from -6 to 6
- stream_tenant_index: int32 [256], P(('rep', 'row')), parts along dimension 0, may hold values from 0 to 511, as said below
- live_block_rows: int32 [8], P(('rep', 'row')), parts along dimension 0, may hold values from 1 to 32
Outputs:
- mixed: bfloat16 [256, 2, 8192], P(('rep', 'row'), None, 'head'), parts along dimension 0
- new_state: bfloat16 [256, 64, 64, 128], P(('rep', 'row'), 'head'), parts along dimension 0
The draws below stay inside these ranges and needn't reach their ends.
There are 2 independent parts, one for each index of `rep`. The reference program is written for one: setup_inputs(seed, part) draws one part's arguments, and reference() takes and returns one part's arrays. A program takes and returns all parts, laid end to end along the dimension named above; an argument that names none is the same for every part. Nothing has to cross between parts.
Inputs may be any that keep to these rules, and one draw needn't show every extreme that they name: `stream_tenant_index`: a stream of block b has a tenant of b * 128 up to (b + 1) * 128 - 1.
All inputs are finite; a program needn't handle non-finite values.
Results may differ from the reference program's by a relative error of at most 0.02.
Values may be sent and summed in bfloat16 or wider, within the bound.
A program may use at most 128 MiB of HBM per device.

```python
import math
import jax
import jax.numpy as jnp
from jax import lax

MODEL_WIDTH = 8192
HEADS = 64
HEAD_P = 64
STATE_N = 128
ADAPTER_RANK = 16
ADAPTER_COUNT = 512
POS = 2
S_DEV = 32
STREAMS = 128
INNER_WIDTH = 4096
N_HEAD = 4


def draw_stream_tenant_index(key, part):
    key_low, key_high = jax.random.split(jax.random.fold_in(key, 11))
    blocks = STREAMS // S_DEV
    per_block = ADAPTER_COUNT // blocks
    first = jax.random.randint(key_low, (STREAMS,), 0, per_block)
    second = jax.random.randint(key_high, (STREAMS,), 0, per_block)
    local = jnp.minimum(first, second)
    block = jnp.arange(STREAMS) // S_DEV
    tenants = block * per_block + local
    tenants = tenants.at[0].set(0).at[STREAMS - 1].set(ADAPTER_COUNT - 1)
    return tenants.astype(jnp.int32)


def draw_live_block_rows(key, part):
    key_low, key_high = jax.random.split(jax.random.fold_in(key, 23))
    blocks = STREAMS // S_DEV
    counts = jax.random.randint(key_low, (blocks,), 1, S_DEV + 1)
    fullest = jax.random.randint(key_high, (), 0, blocks)
    counts = counts.at[fullest].set(S_DEV)
    return counts.astype(jnp.int32)


def spiked(values, own_key, source, target, blocks, factor):
    def block_of(axis_at):
        return (jnp.arange(values.shape[axis_at]) // (values.shape[axis_at] // blocks)).reshape((-1,) + (1,) * (values.ndim - 1 - axis_at))

    near = jax.random.permutation(own_key, blocks)[block_of(target)]
    far = (block_of(target) + blocks // 2) % blocks
    return jnp.where((block_of(source) == near) | (block_of(source) == far), factor * values, values)


def steps_of(key, extent, pieces, least, top_value):
    gain = 1.0
    for dim, shards_of in pieces:
        draws = jax.random.uniform(jax.random.fold_in(jax.random.fold_in(key, 6), dim), (shards_of,), jnp.float32, least / len(pieces), top_value / len(pieces))
        gain = gain * jnp.repeat(jnp.exp(draws), extent[dim] // shards_of).reshape((-1,) + (1,) * (len(extent) - 1 - dim))
    return gain


def centred(key, dims, width, limit, shards=(), dtype=jnp.bfloat16):
    loudness = steps_of(key, dims, shards, -0.22, 0.18) if shards else 1.0
    drawn = jax.random.normal(key, dims, jnp.float32) * width * loudness
    return jnp.minimum(jnp.maximum(drawn, -limit), limit).astype(dtype)


def noise_with(own_key, extent, scale, bound, cuts, heavy, kind=jnp.bfloat16):
    values = scale * jax.random.normal(own_key, extent, jnp.float32)
    if cuts:
        values = values * steps_of(own_key, extent, cuts, -0.22, 0.18)
    return jnp.clip(spiked(values, jax.random.fold_in(own_key, 3), *heavy), -bound, bound).astype(kind)


def setup_inputs(seed: int = 0, part: int = 0) -> dict:
    keys = jax.random.split(jax.random.key(seed), 17)
    part_splits = jax.random.split(jax.random.fold_in(keys[16], part), 17)
    return {
        "hidden": centred(part_splits[0], (STREAMS, POS, MODEL_WIDTH), 1.0, 6.0, ((0, 4), (2, 4))),
        "input_norm_scale": jnp.clip(1.0 + 0.1 * jax.random.normal(keys[1], (MODEL_WIDTH,), jnp.float32), 0.5, 1.5),
        "projection_signal": centred(keys[2], (MODEL_WIDTH, INNER_WIDTH), MODEL_WIDTH ** -0.5, 0.0625, ((0, 4), (1, 4))),
        "projection_gate": centred(keys[3], (MODEL_WIDTH, INNER_WIDTH), MODEL_WIDTH ** -0.5, 0.0625, ((0, 4), (1, 4))),
        "projection_step": centred(keys[4], (MODEL_WIDTH, HEADS), MODEL_WIDTH ** -0.5, 0.0625, ((0, 4), (1, 4))),
        "projection_input_output": centred(keys[5], (MODEL_WIDTH, 2 * STATE_N), MODEL_WIDTH ** -0.5, 0.0625, ((0, 4),)),
        "step_bias": jnp.clip(-4.0 + 4.0 * jax.random.uniform(keys[6], (HEADS,), jnp.float32) ** steps_of(keys[6], (HEADS,), ((0, 4),), -0.2, 0.2), -4.0, 0.0),
        "head_decay_rate": jnp.clip(jnp.exp(math.log(16.0) - 3.465736 * jax.random.uniform(keys[7], (HEADS,), jnp.float32) ** steps_of(keys[7], (HEADS,), ((0, 4),), -0.2, 0.2)), 0.5, 16.0),
        "head_skip_weight": jnp.clip(0.5 + 1.0 * jax.random.uniform(keys[8], (HEADS,), jnp.float32) ** steps_of(keys[8], (HEADS,), ((0, 4),), -0.2, 0.2), 0.5, 1.5),
        "gated_norm_scale": jnp.clip(1.0 + 0.1 * jax.random.normal(keys[9], (INNER_WIDTH,), jnp.float32), 0.5, 1.5),
        "adapter_down_weight": centred(keys[10], (ADAPTER_COUNT, MODEL_WIDTH, ADAPTER_RANK), MODEL_WIDTH ** -0.5, 0.0625, ((0, 4), (1, 4))),
        "adapter_up_weight": centred(keys[11], (ADAPTER_COUNT, ADAPTER_RANK, INNER_WIDTH), ADAPTER_RANK ** -0.5, 1.5, ((0, 4), (2, 4))),
        "output_weight": noise_with(keys[12], (INNER_WIDTH, MODEL_WIDTH), INNER_WIDTH ** -0.5, 0.125, ((0, 4),), (0, 1, 4, 2.0)),
        "scan_state": centred(part_splits[13], (STREAMS, HEADS, HEAD_P, STATE_N), 1.0, 6.0, ((0, 4), (1, 4))),
        "stream_tenant_index": draw_stream_tenant_index(jax.random.fold_in(jax.random.fold_in(keys[16], part), 71), part),
        "live_block_rows": draw_live_block_rows(jax.random.fold_in(jax.random.fold_in(keys[16], part), 71), part),
    }


def reference(hidden, input_norm_scale, projection_signal, projection_gate, projection_step, projection_input_output, step_bias, head_decay_rate, head_skip_weight, gated_norm_scale, adapter_down_weight, adapter_up_weight, output_weight, scan_state, stream_tenant_index, live_block_rows):
    epsilon = 1e-05
    wide = hidden.astype(jnp.float32)
    inverse = lax.rsqrt(lax.optimization_barrier(jnp.sum(wide * wide, -1)) / MODEL_WIDTH + epsilon)
    scaled = (wide * input_norm_scale).astype(jnp.bfloat16)
    down_weight_rows = adapter_down_weight[stream_tenant_index].astype(jnp.float32)
    lowrank = (jnp.einsum('spd,sdr->spr', scaled.astype(jnp.float32), down_weight_rows) * inverse[..., None]).astype(jnp.bfloat16)
    normed = (wide * input_norm_scale * inverse[..., None]).astype(jnp.bfloat16)
    flat = normed.reshape(STREAMS * POS, MODEL_WIDTH)
    xin = jnp.dot(flat, projection_signal, preferred_element_type=jnp.float32).reshape(STREAMS, POS, INNER_WIDTH)
    zin = jnp.dot(flat, projection_gate, preferred_element_type=jnp.float32).reshape(STREAMS, POS, INNER_WIDTH)
    dtin = jnp.dot(flat, projection_step, preferred_element_type=jnp.float32).reshape(STREAMS, POS, HEADS)
    bcin = jnp.dot(flat, projection_input_output, preferred_element_type=jnp.float32).reshape(STREAMS, POS, 2 * STATE_N)
    up_weight_rows = adapter_up_weight[stream_tenant_index].astype(jnp.float32)
    signal = jax.nn.silu(xin + jnp.einsum('spr,srk->spk', lowrank.astype(jnp.float32), up_weight_rows))
    bgate = jax.nn.silu(bcin[..., :STATE_N])
    cgate = jax.nn.silu(bcin[..., STATE_N:])
    steps_dt = jax.nn.softplus(dtin + step_bias)
    decay = jnp.exp(-steps_dt * head_decay_rate)
    index = jnp.arange(STREAMS)
    live = index % S_DEV < live_block_rows[index // S_DEV]
    signal_heads = signal.reshape(STREAMS, POS, HEADS, HEAD_P)

    def one_head(inputs):
        state_head, decay_head, dt_head, signal_head, skip_head = inputs
        carried = state_head.astype(jnp.float32)
        outputs = []
        for position in range(POS):
            updated = carried * decay_head[:, position, None, None] + (dt_head[:, position, None] * signal_head[:, position])[:, :, None] * bgate[:, position, None, :]
            carried = jnp.where(live[:, None, None], updated, carried)
            outputs.append(lax.optimization_barrier(jnp.sum(carried * cgate[:, position, None, :], -1)) + skip_head * signal_head[:, position])
        return (carried.astype(jnp.bfloat16), jnp.stack(outputs, 1))
    states, outputs = lax.map(one_head, (jnp.moveaxis(scan_state, 1, 0), jnp.moveaxis(decay, 2, 0), jnp.moveaxis(steps_dt, 2, 0), jnp.moveaxis(signal_heads, 2, 0), head_skip_weight))
    new_state = jnp.moveaxis(states, 0, 1)
    result = jnp.moveaxis(outputs, 0, 2).reshape(STREAMS, POS, INNER_WIDTH)
    gated = result * jax.nn.silu(zin)
    outnorm = (gated * lax.rsqrt(lax.optimization_barrier(jnp.mean(gated * gated, -1)) + epsilon)[..., None] * gated_norm_scale).astype(jnp.bfloat16)
    out_flat = outnorm.reshape(STREAMS * POS, INNER_WIDTH)
    group_width = INNER_WIDTH // N_HEAD
    total = jnp.zeros((STREAMS * POS, MODEL_WIDTH), jnp.float32)
    for group in range(N_HEAD):
        part = jnp.dot(out_flat[:, group * group_width:(group + 1) * group_width], output_weight[group * group_width:(group + 1) * group_width], preferred_element_type=jnp.float32).astype(jnp.bfloat16)
        part = lax.optimization_barrier(part)
        total = total + part.astype(jnp.float32)
    mixer = total.reshape(STREAMS, POS, MODEL_WIDTH)
    mixed = (wide + jnp.where(live[:, None, None], mixer, 0.0)).astype(jnp.bfloat16)
    return (mixed, new_state)
```

```python
import functools

import jax
import jax.numpy as jnp
from jax import lax
from jax.experimental import pallas as pl
from jax.experimental.pallas import tpu as pltpu
from jax.sharding import PartitionSpec as P

EPSILON = 1e-05
GROUP = 4
BF16 = jnp.bfloat16
F32 = jnp.float32
MESH = pl.DeviceIdType.MESH
LIMIT = 48 * 1024 * 1024
ANY = pl.BlockSpec(memory_space=pl.ANY)
VM = pl.BlockSpec(memory_space=pltpu.VMEM)
SM = pl.BlockSpec(memory_space=pltpu.SMEM)


def nt(a, b):
    return lax.dot_general(a, b, (((1,), (1,)), ((), ())), preferred_element_type=F32)


def split2(a):
    high = a.astype(BF16)
    return high, (a - high.astype(F32)).astype(BF16)


def front_kernel(index_ref, hidden_ref, scale_ref, *rest):
    downs, (scaled_ref, stats_ref) = rest[:GROUP], rest[GROUP:]
    rank = downs[0].shape[1]
    wide = hidden_ref[...].astype(F32)
    scaled = (wide * scale_ref[...]).astype(BF16)
    scaled_ref[...] = scaled
    rows = scaled.shape[0]
    positions = rows // GROUP
    squares = jnp.sum(wide * wide, -1, keepdims=True)
    stack = jnp.concatenate([d[0] for d in downs], axis=0)
    low = nt(scaled, stack)
    row = lax.broadcasted_iota(jnp.int32, low.shape, 0) // positions
    col = lax.broadcasted_iota(jnp.int32, low.shape, 1) // rank
    low = jnp.where(row == col, low, 0.0)
    filler = stats_ref.shape[1] - low.shape[1]
    stats_ref[...] = jnp.concatenate([low, jnp.broadcast_to(squares, (rows, filler))], axis=1)


def front(hidden, scale, down, index, positions):
    tokens, width = hidden.shape
    capacity, rank, _ = down.shape
    rows = GROUP * positions

    def down_spec(j):
        return pl.BlockSpec(
            (1, rank, width), lambda g, idx: (lax.rem(idx[g * GROUP + j], capacity), 0, 0)
        )

    return pl.pallas_call(
        front_kernel,
        grid_spec=pltpu.PrefetchScalarGridSpec(
            num_scalar_prefetch=1,
            grid=(tokens // rows,),
            in_specs=[
                pl.BlockSpec((rows, width), lambda g, idx: (g, 0)),
                pl.BlockSpec((1, width), lambda g, idx: (0, 0)),
            ]
            + [down_spec(j) for j in range(GROUP)],
            out_specs=[
                pl.BlockSpec((rows, width), lambda g, idx: (g, 0)),
                pl.BlockSpec((rows, 128), lambda g, idx: (g, 0)),
            ],
        ),
        out_shape=[
            jax.ShapeDtypeStruct((tokens, width), BF16),
            jax.ShapeDtypeStruct((tokens, 128), F32),
        ],
        name="front",
    )(index, hidden, scale.reshape(1, -1), *([down] * GROUP))


def project_kernel(
    heads, rows, model_width, scaled_ref, stats_ref, wsig_ref, wgate_ref, wstep_ref, wbc_ref,
    proj_ref, low_ref,
    wsig, wgate, wstep, wbc, xbuf, pbuf, rbuf, sbuf,
    w_sem, self_sem, send_a, recv_a, send_b, recv_b, send_s, recv_s, send_r, recv_r,
):
    h = lax.axis_index("head")
    r = lax.axis_index("row")
    tokens, width = scaled_ref.shape
    share = heads // rows
    pieces = min(heads, tokens // 16)
    every = heads // pieces
    prow = tokens // pieces
    inner = wsig.shape[1]
    heads_here = wstep.shape[0]
    loads = [
        pltpu.make_async_copy(s, d, w_sem.at[i])
        for i, (s, d) in enumerate(
            [(wbc_ref, wbc), (wstep_ref, wstep), (wsig_ref, wsig), (wgate_ref, wgate)]
        )
    ]
    for load in loads:
        load.start()
    target_row = h // share
    piece = h // every

    def when(condition):
        return (lambda f: f()) if condition is True else pl.when(condition)

    is_owner = True if every == 1 else (lax.rem(h, every) == 0)

    barrier = pltpu.get_barrier_semaphore()
    for d in range(1, heads):
        pl.semaphore_signal(
            barrier, inc=1, device_id={"head": lax.rem(h + d, heads)}, device_id_type=MESH
        )
    for d in range(1, rows):
        pl.semaphore_signal(
            barrier, inc=1, device_id={"row": lax.rem(r + d, rows)}, device_id_type=MESH
        )

    @when(is_owner)
    def _():
        for j in range(share):
            for e in range(rows):
                src_h = r * share + j
                src_r = lax.rem(r + e, rows)
                same = jnp.logical_and(src_h == h, src_r == r)

                @pl.when(jnp.logical_not(same))
                def _():
                    pl.semaphore_signal(
                        barrier, inc=1, device_id={"head": src_h, "row": src_r},
                        device_id_type=MESH,
                    )

    to_self = jnp.logical_and(lax.rem(h, every) == 0, target_row == r).astype(jnp.int32)
    pl.semaphore_wait(barrier, heads - 1 + rows - 1 + pieces - to_self)

    def a_parts(k):
        src = scaled_ref.at[pl.ds(k * prow, prow), :]
        row0 = pl.multiple_of(r * tokens + k * prow, 16)
        col0 = pl.multiple_of(lax.rem(h, share) * width, 128)
        return src, xbuf.at[pl.ds(row0, prow), pl.ds(col0, width)]

    def a_remote(k):
        src, dst = a_parts(k)
        return pltpu.make_async_remote_copy(
            src_ref=src, dst_ref=dst, send_sem=send_a.at[k],
            recv_sem=recv_a.at[r * share + lax.rem(h, share)],
            device_id={"head": k * every, "row": target_row}, device_id_type=MESH,
        )

    def a_same(k):
        return jnp.logical_and(h == k * every, target_row == r)

    for k in range(pieces):
        @pl.when(jnp.logical_not(a_same(k)))
        def _():
            a_remote(k).start()

        @pl.when(a_same(k))
        def _():
            src, dst = a_parts(k)
            pltpu.make_async_copy(src, dst, recv_a.at[r * share + lax.rem(h, share)]).start()

    stat_copies = []
    for d in range(1, heads):
        copy = pltpu.make_async_remote_copy(
            src_ref=stats_ref, dst_ref=sbuf.at[d], send_sem=send_s.at[d], recv_sem=recv_s.at[d],
            device_id={"head": lax.rem(h + d, heads)}, device_id_type=MESH,
        )
        copy.start()
        stat_copies.append(copy)

    pbuf[:, 2 * inner + wbc.shape[1] :] = jnp.zeros((rows * tokens, 128), BF16)

    def block_rows(e, k):
        row0 = lax.rem(r + e, rows) * tokens + k * prow
        return xbuf.at[pl.ds(pl.multiple_of(row0, 16), prow), :]

    def b_copy(d, e, k):
        return pltpu.make_async_remote_copy(
            src_ref=block_rows(e, k), dst_ref=block_rows(e, k),
            send_sem=send_b.at[d, e], recv_sem=recv_b.at[d, e],
            device_id={"head": lax.rem(h + d, heads)}, device_id_type=MESH,
        )

    @when(is_owner)
    def _():
        for e in range(rows):
            src_r = lax.rem(r + e, rows)
            for j in range(share):
                dst = xbuf.at[
                    pl.ds(pl.multiple_of(src_r * tokens + piece * prow, 16), prow),
                    pl.ds(j * width, width),
                ]
                pltpu.make_async_copy(dst, dst, recv_a.at[src_r * share + j]).wait()
            for d in range(1, heads):
                b_copy(d, e, piece).start()

    for e in range(rows):
        for d in range(1, heads):
            from_h = lax.rem(h - d + heads, heads)

            @when(True if every == 1 else lax.rem(from_h, every) == 0)
            def _():
                b_copy(d, e, from_h // every).wait_recv()

    bc_width = wbc.shape[1]
    half = min(inner, 512)
    chunks = [(wbc, 0, bc_width, 2 * inner, 0), (wstep, None, 128, 2 * inner + bc_width, 1)]
    for i, w in ((2, wsig), (3, wgate)):
        for c in range(0, inner, half):
            chunks.append((w, c, half, (i - 2) * inner + c, i))
    r_copies = []
    waited = set()
    for n, (w, c, cw, out, load) in enumerate(chunks):
        if load not in waited:
            loads[load].wait()
            waited.add(load)
        if c is None:
            pbuf[:, out : out + heads_here] = nt(xbuf[...], w[...]).astype(BF16)
        else:
            pbuf[:, out : out + cw] = jnp.dot(
                xbuf[...], w[:, c : c + cw], preferred_element_type=F32
            ).astype(BF16)
        for d in range(1, rows):
            to = lax.rem(r + d, rows)
            copy = pltpu.make_async_remote_copy(
                src_ref=pbuf.at[pl.ds(pl.multiple_of(to * tokens, 16), tokens), out : out + cw],
                dst_ref=rbuf.at[d, :, out : out + cw],
                send_sem=send_r.at[d, n], recv_sem=recv_r.at[d, n],
                device_id={"row": to}, device_id_type=MESH,
            )
            copy.start()
            r_copies.append((n, copy))

    total = stats_ref[...]
    for d in range(1, heads):
        stat_copies[d - 1].wait_recv()
        total = total + sbuf[d]
    inverse = lax.rsqrt(total[:, 127:128] / model_width + EPSILON)
    low_ref[...] = total * inverse
    own = pl.ds(pl.multiple_of(r * tokens, 16), tokens)
    for n, (w, c, cw, out, load) in enumerate(chunks):
        for m, copy in r_copies:
            if m == n:
                copy.wait_recv()
        part = pbuf[own, out : out + cw].astype(F32)
        for d in range(1, rows):
            part = part + rbuf[d, :, out : out + cw].astype(F32)
        proj_ref[:, out : out + cw] = part * inverse

    for _, copy in r_copies:
        copy.wait_send()
    for copy in stat_copies:
        copy.wait_send()
    for k in range(pieces):
        @pl.when(jnp.logical_not(a_same(k)))
        def _():
            a_remote(k).wait_send()

    @when(is_owner)
    def _():
        for e in range(rows):
            for d in range(1, heads):
                b_copy(d, e, piece).wait_send()


def project(scaled, stats, wsig, wgate, wstep, wbc, heads, rows):
    tokens, width = scaled.shape
    depth, inner = wsig.shape
    out_width = 2 * inner + wbc.shape[1] + 128
    share = heads // rows
    pieces = min(heads, tokens // 16)
    n_chunks = 2 + 2 * (inner // min(inner, 512))
    dma = pltpu.SemaphoreType.DMA
    return pl.pallas_call(
        functools.partial(project_kernel, heads, rows, float(width * heads)),
        out_shape=[
            jax.ShapeDtypeStruct((tokens, out_width), F32),
            jax.ShapeDtypeStruct((tokens, 128), F32),
        ],
        in_specs=[VM, VM, ANY, ANY, ANY, ANY],
        out_specs=[VM, VM],
        scratch_shapes=[
            pltpu.VMEM(wsig.shape, BF16),
            pltpu.VMEM(wgate.shape, BF16),
            pltpu.VMEM(wstep.shape, BF16),
            pltpu.VMEM(wbc.shape, BF16),
            pltpu.VMEM((rows * tokens, depth), BF16),
            pltpu.VMEM((rows * tokens, out_width), BF16),
            pltpu.VMEM((rows, tokens, out_width), BF16),
            pltpu.VMEM((heads, tokens, 128), F32),
            dma((4,)),
            dma((1,)),
            dma((pieces,)),
            dma((rows * share,)),
            dma((heads, rows)),
            dma((heads, rows)),
            dma((heads,)),
            dma((heads,)),
            dma((rows, n_chunks)),
            dma((rows, n_chunks)),
        ],
        compiler_params=pltpu.CompilerParams(
            collective_id=0, has_side_effects=True, vmem_limit_bytes=LIMIT
        ),
        name="project",
    )(scaled, stats, wsig, wgate, wstep, wbc)


def scan_kernel(
    positions, index_ref, live_ref, proj_ref, low_ref, bias_ref, rate_ref, skip_ref, gain_ref,
    spread_ref, state_ref, *rest
):
    ups, (new_ref, gated_ref, sq_ref) = rest[:GROUP], rest[GROUP:]
    g = pl.program_id(0)
    rows = proj_ref.shape[0]
    inner = ups[0].shape[2]
    rank = ups[0].shape[1]
    n_state = state_ref.shape[3]
    shape_state = state_ref.shape[1:]
    base = 2 * inner
    xin = proj_ref[:, :inner]
    zin = proj_ref[:, inner:base]
    bc = proj_ref[:, base : base + 2 * n_state]
    dtin = proj_ref[:, base + 2 * n_state :]
    low = low_ref[:, : GROUP * rank].astype(BF16)
    up = jnp.concatenate([u[0] for u in ups], axis=0)
    x = jax.nn.silu(xin + jnp.dot(low, up, preferred_element_type=F32))
    bgate = jax.nn.silu(bc[:, :n_state])
    cgate = jax.nn.silu(bc[:, n_state:])
    row1 = lax.broadcasted_iota(jnp.int32, (rows, 1), 0)
    stream1 = row1 // positions
    live = (g * GROUP + stream1) < live_ref[0]
    dt = jax.nn.softplus(dtin + bias_ref[...])
    decay = jnp.exp(-dt * rate_ref[...])
    dt_high, dt_low = split2(dt)
    de_high, de_low = split2(decay)
    spread = jnp.dot(
        jnp.concatenate([dt_high, dt_low, de_high, de_low], axis=0), spread_ref[...],
        preferred_element_type=F32,
    )
    dt_wide = spread[:rows] + spread[rows : 2 * rows]
    de_wide = spread[2 * rows : 3 * rows] + spread[3 * rows :]
    u = jnp.where(live, dt_wide * x, 0.0)
    de_wide = jnp.where(live, de_wide, 1.0)

    second = lax.rem(row1, positions) == 1
    prev_de = pltpu.roll(de_wide, 1, 0)
    prev_u = pltpu.roll(u, 1, 0)
    prev_b = pltpu.roll(bgate, 1, 0)
    keep = jnp.where(second, de_wide * prev_de, de_wide)
    carried_u = jnp.where(second, u, u * pltpu.roll(de_wide, rows - 1, 0))
    keep_high, keep_low = split2(keep)
    left = jnp.concatenate(
        [carried_u.astype(BF16), keep_high, keep_low, jnp.zeros_like(keep_low)], axis=0
    )
    left = left.T
    y = jnp.zeros((rows, inner), F32)
    zero_b = jnp.zeros((rows, n_state), F32)
    for j in range(GROUP):
        mine = stream1 == j
        b_mine = jnp.where(mine, bgate, 0.0)
        ones_mine = jnp.broadcast_to(jnp.where(mine & second, 1.0, 0.0), (rows, n_state))
        right = jnp.concatenate(
            [
                jnp.concatenate([b_mine, zero_b], axis=1),
                jnp.concatenate([zero_b, ones_mine], axis=1),
                jnp.concatenate([zero_b, ones_mine], axis=1),
                jnp.concatenate([zero_b, zero_b], axis=1),
            ],
            axis=0,
        ).astype(BF16)
        state = state_ref[j].reshape(inner, n_state)
        both = jnp.dot(left, right, preferred_element_type=F32)
        new = state.astype(F32) * both[:, n_state:] + both[:, :n_state]
        new_ref[j] = new.astype(BF16).reshape(shape_state)
        y = y + nt(jnp.where(mine, cgate, 0.0).astype(BF16), state)

    dot_own = jnp.sum(bgate * cgate, -1, keepdims=True)
    dot_prev = jnp.sum(prev_b * cgate, -1, keepdims=True)
    y = keep * y + u * dot_own + jnp.where(second, de_wide * prev_u * dot_prev, 0.0)
    y = y + skip_ref[...] * x
    gated = y * jax.nn.silu(zin)
    gated_ref[...] = (gated * gain_ref[...]).astype(BF16)
    sq_ref[...] = jnp.broadcast_to(jnp.sum(gated * gated, -1, keepdims=True), sq_ref.shape)


def scan(index, live, proj, low, bias, rate, skip, gain, state, up, positions):
    tokens, out_width = proj.shape
    capacity, rank, inner = up.shape
    rows = GROUP * positions
    heads_here = bias.shape[0]
    head_size = inner // heads_here
    spread = (jnp.arange(128)[:, None] == jnp.arange(inner)[None, :] // head_size).astype(BF16)
    pad = ((0, 0), (0, 128 - heads_here))
    bias = jnp.pad(bias.reshape(1, -1), pad)
    rate = jnp.pad(rate.reshape(1, -1), pad)
    skip = jnp.repeat(skip, head_size).reshape(1, -1)

    def up_spec(j):
        return pl.BlockSpec(
            (1, rank, inner), lambda g, idx, lv: (lax.rem(idx[g * GROUP + j], capacity), 0, 0)
        )

    def whole(a):
        return pl.BlockSpec(a.shape, lambda g, idx, lv: (0, 0))

    def by_rows(w):
        return pl.BlockSpec((rows, w), lambda g, idx, lv: (g, 0))

    gain = gain.reshape(1, -1)
    state_spec = pl.BlockSpec((GROUP,) + state.shape[1:], lambda g, idx, lv: (g, 0, 0, 0))
    return pl.pallas_call(
        functools.partial(scan_kernel, positions),
        grid_spec=pltpu.PrefetchScalarGridSpec(
            num_scalar_prefetch=2,
            grid=(tokens // rows,),
            in_specs=[by_rows(out_width), by_rows(128), whole(bias), whole(rate), whole(skip),
                      whole(gain), whole(spread), state_spec]
            + [up_spec(j) for j in range(GROUP)],
            out_specs=[state_spec, by_rows(inner), by_rows(128)],
        ),
        out_shape=[
            jax.ShapeDtypeStruct(state.shape, BF16),
            jax.ShapeDtypeStruct((tokens, inner), BF16),
            jax.ShapeDtypeStruct((tokens, 128), F32),
        ],
        compiler_params=pltpu.CompilerParams(vmem_limit_bytes=LIMIT),
        name="scan",
    )(index, live, proj, low, bias, rate, skip, gain, spread, state, *([up] * GROUP))


def output_kernel(
    heads, positions, inner_width, live_ref, gated_ref, sq_ref, hidden_ref, w_ref, out_ref,
    wbuf, pbuf, rbuf, sbuf, w_sem, send_s, recv_s, send_r, recv_r,
):
    h = lax.axis_index("head")
    tokens, width = hidden_ref.shape
    order = [d for d in range(1, heads)] + [0]
    order = sorted(order, key=lambda d: (d == 0, abs(d - heads // 2)))

    def load(d):
        to = lax.rem(h + d, heads)
        return pltpu.make_async_copy(
            w_ref.at[:, pl.ds(pl.multiple_of(to * width, 128), width)], wbuf.at[d], w_sem.at[d]
        )

    for d in order:
        load(d).start()
    barrier = pltpu.get_barrier_semaphore()
    for d in range(1, heads):
        pl.semaphore_signal(
            barrier, inc=1, device_id={"head": lax.rem(h + d, heads)}, device_id_type=MESH
        )
    pl.semaphore_wait(barrier, heads - 1)
    copies = []
    for d in range(1, heads):
        copy = pltpu.make_async_remote_copy(
            src_ref=sq_ref, dst_ref=sbuf.at[d], send_sem=send_s.at[d], recv_sem=recv_s.at[d],
            device_id={"head": lax.rem(h + d, heads)}, device_id_type=MESH,
        )
        copy.start()
        copies.append(copy)
    parts = {}
    step = min(width, 512)
    for d in order:
        load(d).wait()
        for c in range(0, width, step):
            pbuf[d, :, c : c + step] = jnp.dot(
                gated_ref[...], wbuf[d, :, c : c + step], preferred_element_type=F32
            ).astype(BF16)
        if d:
            copy = pltpu.make_async_remote_copy(
                src_ref=pbuf.at[d], dst_ref=rbuf.at[d], send_sem=send_r.at[d],
                recv_sem=recv_r.at[d],
                device_id={"head": lax.rem(h + d, heads)}, device_id_type=MESH,
            )
            copy.start()
            parts[d] = copy
    square = sq_ref[...]
    for d in range(1, heads):
        copies[d - 1].wait_recv()
        square = square + sbuf[d]
    inverse = lax.rsqrt(square[:, :1] / inner_width + EPSILON)
    mixer = pbuf[0].astype(F32)
    for d in sorted(parts, key=lambda d: -abs(d - heads // 2)):
        parts[d].wait_recv()
        mixer = mixer + rbuf[d].astype(F32)
    stream = lax.broadcasted_iota(jnp.int32, (tokens, 1), 0) // positions
    live = stream < live_ref[0]
    out_ref[...] = (
        hidden_ref[...].astype(F32) + jnp.where(live, mixer * inverse, 0.0)
    ).astype(BF16)
    for copy in copies:
        copy.wait_send()
    for copy in parts.values():
        copy.wait_send()


def output(live, gated, sq, hidden, weight, heads, positions):
    tokens, width = hidden.shape
    inner = gated.shape[1]
    dma = pltpu.SemaphoreType.DMA
    return pl.pallas_call(
        functools.partial(output_kernel, heads, positions, float(inner * heads)),
        out_shape=jax.ShapeDtypeStruct((tokens, width), BF16),
        in_specs=[SM, VM, VM, VM, ANY],
        out_specs=VM,
        scratch_shapes=[
            pltpu.VMEM((heads, inner, width), BF16),
            pltpu.VMEM((heads, tokens, width), BF16),
            pltpu.VMEM((heads, tokens, width), BF16),
            pltpu.VMEM((heads, tokens, 128), F32),
            dma((heads,)),
            dma((heads,)),
            dma((heads,)),
            dma((heads,)),
            dma((heads,)),
        ],
        compiler_params=pltpu.CompilerParams(
            collective_id=1, has_side_effects=True, vmem_limit_bytes=LIMIT
        ),
        name="output",
    )(live, gated, sq, hidden, weight)


def on_device(
    heads, rows,
    hidden, input_norm_scale, projection_signal, projection_gate, projection_step,
    projection_input_output, step_bias, head_decay_rate, head_skip_weight, gated_norm_scale,
    adapter_down_weight, adapter_up_weight, output_weight, scan_state, stream_tenant_index,
    live_block_rows,
):
    streams, positions, width = hidden.shape
    flat = hidden.reshape(streams * positions, width)
    down = jnp.swapaxes(adapter_down_weight, 1, 2)
    scaled, stats = front(flat, input_norm_scale, down, stream_tenant_index, positions)
    proj, low = project(
        scaled, stats, projection_signal, projection_gate, projection_step.T,
        projection_input_output, heads, rows,
    )
    new_state, gated, sq = scan(
        stream_tenant_index, live_block_rows, proj, low, step_bias, head_decay_rate,
        head_skip_weight, gated_norm_scale, scan_state, adapter_up_weight, positions,
    )
    mixed = output(live_block_rows, gated, sq, flat, output_weight, heads, positions)
    return mixed.reshape(hidden.shape), new_state


def solution(mesh):
    in_specs = (
        P(("rep", "row"), None, "head"),
        P("head"),
        P("row", "head"),
        P("row", "head"),
        P("row", "head"),
        P("row", None),
        P("head"),
        P("head"),
        P("head"),
        P("head"),
        P("row", "head", None),
        P("row", None, "head"),
        P("head", None),
        P(("rep", "row"), "head", None, None),
        P(("rep", "row")),
        P(("rep", "row")),
    )
    out_specs = (P(("rep", "row"), None, "head"), P(("rep", "row"), "head", None, None))
    return jax.shard_map(
        functools.partial(on_device, mesh.shape["head"], mesh.shape["row"]),
        mesh=mesh, in_specs=in_specs, out_specs=out_specs, check_vma=False,
    )
```

```python
import functools

import jax
import jax.numpy as jnp
from jax import lax
from jax.experimental import pallas as pl
from jax.experimental.pallas import tpu as pltpu
from jax.sharding import PartitionSpec as P

EPSILON = 1e-05
GROUP = 4
BF16 = jnp.bfloat16
F32 = jnp.float32
MESH = pl.DeviceIdType.MESH
LIMIT = 48 * 1024 * 1024
ANY = pl.BlockSpec(memory_space=pl.ANY)
VM = pl.BlockSpec(memory_space=pltpu.VMEM)
SM = pl.BlockSpec(memory_space=pltpu.SMEM)


def nt(a, b):
    return lax.dot_general(a, b, (((1,), (1,)), ((), ())), preferred_element_type=F32)


def split2(a):
    high = a.astype(BF16)
    return high, (a - high.astype(F32)).astype(BF16)


def front_kernel(
    capacity, positions, index_ref, hidden_ref, scale_ref, down_ref, scaled_ref, stats_ref,
    dbuf, sems,
):
    tokens = hidden_ref.shape[0]
    rank = down_ref.shape[1]
    copies = []
    for s in range(tokens // positions):
        copy = pltpu.make_async_copy(
            down_ref.at[lax.rem(index_ref[s], capacity)],
            dbuf.at[s * rank : (s + 1) * rank, :], sems.at[s],
        )
        copy.start()
        copies.append(copy)
    wide = hidden_ref[...].astype(F32)
    scaled_ref[...] = (wide * scale_ref[...]).astype(BF16)
    squares = jnp.sum(wide * wide, -1, keepdims=True)
    streams = 2 * GROUP
    rows = streams * positions
    lanes = streams * rank
    row = lax.broadcasted_iota(jnp.int32, (rows, lanes), 0) // positions
    col = lax.broadcasted_iota(jnp.int32, (rows, lanes), 1) // rank
    for g in range(tokens // rows):
        for copy in copies[g * streams : (g + 1) * streams]:
            copy.wait()
        here = slice(g * rows, (g + 1) * rows)
        low = nt(scaled_ref[here, :], dbuf[g * lanes : (g + 1) * lanes, :])
        low = jnp.where(row < GROUP, low, pltpu.roll(low, lanes // 2, 1))
        low = jnp.where(lax.rem(row, GROUP) == col, low, 0.0)
        stats_ref[here, :] = jnp.where(col < GROUP, low, squares[here, :])


def front(hidden, scale, down, index, positions):
    tokens, width = hidden.shape
    capacity, rank, _ = down.shape
    streams = tokens // positions
    return pl.pallas_call(
        functools.partial(front_kernel, capacity, positions),
        in_specs=[SM, VM, VM, ANY],
        out_specs=[VM, VM],
        out_shape=[
            jax.ShapeDtypeStruct((tokens, width), BF16),
            jax.ShapeDtypeStruct((tokens, 128), F32),
        ],
        scratch_shapes=[
            pltpu.VMEM((streams * rank, width), BF16),
            pltpu.SemaphoreType.DMA((streams,)),
        ],
        compiler_params=pltpu.CompilerParams(vmem_limit_bytes=24 * 1024 * 1024),
        name="front",
    )(index, hidden, scale.reshape(1, -1), down)


def project_kernel(
    heads, rows, model_width, scaled_ref, stats_ref, wsig_ref, wgate_ref, wstep_ref, wbc_ref,
    proj_ref, low_ref,
    wsig, wgate, wstep, wbc, xbuf, pbuf, rup, rdown, sbuf,
    w_sem, send_a, recv_a, send_b, recv_b, send_s, recv_s, send_r, recv_u, recv_d,
):
    h = lax.axis_index("head")
    r = lax.axis_index("row")
    tokens, width = scaled_ref.shape
    share = heads // rows
    pieces = min(heads, tokens // 16)
    every = heads // pieces
    prow = tokens // pieces
    inner = wsig.shape[1]
    heads_here = wstep.shape[0]
    loads = [
        pltpu.make_async_copy(s, d, w_sem.at[i])
        for i, (s, d) in enumerate(
            [(wbc_ref, wbc), (wstep_ref, wstep), (wsig_ref, wsig), (wgate_ref, wgate)]
        )
    ]
    for load in loads:
        load.start()
    target_row = h // share
    piece = h // every

    def when(condition):
        return (lambda f: f()) if condition is True else pl.when(condition)

    is_owner = True if every == 1 else (lax.rem(h, every) == 0)

    barrier = pltpu.get_barrier_semaphore()
    for d in range(1, heads):
        pl.semaphore_signal(
            barrier, inc=1, device_id={"head": lax.rem(h + d, heads)}, device_id_type=MESH
        )
    for d in range(1, rows):
        pl.semaphore_signal(
            barrier, inc=1, device_id={"row": lax.rem(r + d, rows)}, device_id_type=MESH
        )

    @when(is_owner)
    def _():
        for j in range(share):
            for e in range(rows):
                src_h = r * share + j
                src_r = lax.rem(r + e, rows)
                same = jnp.logical_and(src_h == h, src_r == r)

                @pl.when(jnp.logical_not(same))
                def _():
                    pl.semaphore_signal(
                        barrier, inc=1, device_id={"head": src_h, "row": src_r},
                        device_id_type=MESH,
                    )

    to_self = jnp.logical_and(lax.rem(h, every) == 0, target_row == r).astype(jnp.int32)
    pl.semaphore_wait(barrier, heads - 1 + rows - 1 + pieces - to_self)

    def a_parts(k):
        src = scaled_ref.at[pl.ds(k * prow, prow), :]
        row0 = pl.multiple_of(r * tokens + k * prow, 16)
        col0 = pl.multiple_of(lax.rem(h, share) * width, 128)
        return src, xbuf.at[pl.ds(row0, prow), pl.ds(col0, width)]

    def a_remote(k):
        src, dst = a_parts(k)
        return pltpu.make_async_remote_copy(
            src_ref=src, dst_ref=dst, send_sem=send_a.at[k],
            recv_sem=recv_a.at[r * share + lax.rem(h, share)],
            device_id={"head": k * every, "row": target_row}, device_id_type=MESH,
        )

    def a_same(k):
        return jnp.logical_and(h == k * every, target_row == r)

    for k in range(pieces):
        @pl.when(jnp.logical_not(a_same(k)))
        def _():
            a_remote(k).start()

        @pl.when(a_same(k))
        def _():
            src, dst = a_parts(k)
            pltpu.make_async_copy(src, dst, recv_a.at[r * share + lax.rem(h, share)]).start()

    stat_copies = []
    for d in range(1, heads):
        copy = pltpu.make_async_remote_copy(
            src_ref=stats_ref, dst_ref=sbuf.at[d], send_sem=send_s.at[d], recv_sem=recv_s.at[d],
            device_id={"head": lax.rem(h + d, heads)}, device_id_type=MESH,
        )
        copy.start()
        stat_copies.append(copy)

    pbuf[:, 2 * inner + wbc.shape[1] :] = jnp.zeros((rows * tokens, 128), BF16)

    def block_rows(e, k):
        row0 = lax.rem(r + e, rows) * tokens + k * prow
        return xbuf.at[pl.ds(pl.multiple_of(row0, 16), prow), :]

    def b_copy(d, e, k):
        return pltpu.make_async_remote_copy(
            src_ref=block_rows(e, k), dst_ref=block_rows(e, k),
            send_sem=send_b.at[d, e], recv_sem=recv_b.at[d, e],
            device_id={"head": lax.rem(h + d, heads)}, device_id_type=MESH,
        )

    @when(is_owner)
    def _():
        for e in range(rows):
            src_r = lax.rem(r + e, rows)
            for j in range(share):
                dst = xbuf.at[
                    pl.ds(pl.multiple_of(src_r * tokens + piece * prow, 16), prow),
                    pl.ds(j * width, width),
                ]
                pltpu.make_async_copy(dst, dst, recv_a.at[src_r * share + j]).wait()
            for d in range(1, heads):
                b_copy(d, e, piece).start()

    for e in range(rows):
        for d in range(1, heads):
            from_h = lax.rem(h - d + heads, heads)

            @when(True if every == 1 else lax.rem(from_h, every) == 0)
            def _():
                b_copy(d, e, from_h // every).wait_recv()

    bc_width = wbc.shape[1]
    half = min(inner, 512)
    chunks = [(wbc, 0, bc_width, 2 * inner, 0), (wstep, None, 128, 2 * inner + bc_width, 1)]
    for i, w in ((2, wsig), (3, wgate)):
        for c in range(0, inner, half):
            chunks.append((w, c, half, (i - 2) * inner + c, i))

    def columns(n):
        return slice(chunks[n][3], chunks[n][3] + chunks[n][2])

    def hop(t, n, up):
        there = lax.rem(r + (1 if up else rows - 1), rows)
        return pltpu.make_async_remote_copy(
            src_ref=pbuf.at[t * tokens : (t + 1) * tokens, columns(n)],
            dst_ref=(rup if up else rdown).at[t, :, columns(n)],
            send_sem=send_r.at[t, n], recv_sem=(recv_u if up else recv_d).at[t, n],
            device_id={"row": there}, device_id_type=MESH,
        )

    def first_hop(n):
        @pl.when(r == 0)
        def _():
            for t in range(rows - 1, 0, -1):
                hop(t, n, True).start()

        @pl.when(r == rows - 1)
        def _():
            for t in range(rows - 1):
                hop(t, n, False).start()

    def pass_on(t, n, up):
        copy = hop(t, n, up)
        copy.wait_recv()
        here = slice(t * tokens, (t + 1) * tokens)
        came = (rup if up else rdown)[t, :, columns(n)]
        pbuf[here, columns(n)] = (
            pbuf[here, columns(n)].astype(F32) + came.astype(F32)
        ).astype(BF16)
        copy.start()

    waited = set()
    for n, (w, c, cw, out, load) in enumerate(chunks):
        if load not in waited:
            loads[load].wait()
            waited.add(load)
        if c is None:
            pbuf[:, out : out + heads_here] = nt(xbuf[...], w[...]).astype(BF16)
        else:
            pbuf[:, out : out + cw] = jnp.dot(
                xbuf[...], w[:, c : c + cw], preferred_element_type=F32
            ).astype(BF16)
        first_hop(n)

    for step in range(len(chunks) + rows - 3):
        for k in range(1, rows - 1):
            n = step - (k - 1)
            if 0 <= n < len(chunks):
                @pl.when(r == k)
                def _():
                    for t in range(rows - 1, k, -1):
                        pass_on(t, n, True)

                @pl.when(r == rows - 1 - k)
                def _():
                    for t in range(rows - 1 - k):
                        pass_on(t, n, False)

    total = stats_ref[...]
    for d in range(1, heads):
        stat_copies[d - 1].wait_recv()
        total = total + sbuf[d]
    inverse = lax.rsqrt(total[:, 127:128] / model_width + EPSILON)
    low_ref[...] = total * inverse
    own = pl.ds(pl.multiple_of(r * tokens, 16), tokens)
    for n in range(len(chunks)):
        proj_ref[:, columns(n)] = pbuf[own, columns(n)].astype(F32)
        for buffer, sem, there in ((rup, recv_u, r > 0), (rdown, recv_d, r < rows - 1)):
            @pl.when(there)
            def _():
                came = buffer.at[r, :, columns(n)]
                pltpu.make_async_copy(came, came, sem.at[r, n]).wait()
                proj_ref[:, columns(n)] = proj_ref[:, columns(n)] + came[...].astype(F32)
        proj_ref[:, columns(n)] = proj_ref[:, columns(n)] * inverse

    for n in range(len(chunks)):
        for t in range(rows):
            @pl.when(t > r)
            def _():
                hop(t, n, True).wait_send()

            @pl.when(t < r)
            def _():
                hop(t, n, False).wait_send()
    for copy in stat_copies:
        copy.wait_send()
    for k in range(pieces):
        @pl.when(jnp.logical_not(a_same(k)))
        def _():
            a_remote(k).wait_send()

    @when(is_owner)
    def _():
        for e in range(rows):
            for d in range(1, heads):
                b_copy(d, e, piece).wait_send()


def project(scaled, stats, wsig, wgate, wstep, wbc, heads, rows):
    tokens, width = scaled.shape
    depth, inner = wsig.shape
    out_width = 2 * inner + wbc.shape[1] + 128
    share = heads // rows
    pieces = min(heads, tokens // 16)
    n_chunks = 2 + 2 * (inner // min(inner, 512))
    dma = pltpu.SemaphoreType.DMA
    return pl.pallas_call(
        functools.partial(project_kernel, heads, rows, float(width * heads)),
        out_shape=[
            jax.ShapeDtypeStruct((tokens, out_width), F32),
            jax.ShapeDtypeStruct((tokens, 128), F32),
        ],
        in_specs=[VM, VM, ANY, ANY, ANY, ANY],
        out_specs=[VM, VM],
        scratch_shapes=[
            pltpu.VMEM(wsig.shape, BF16),
            pltpu.VMEM(wgate.shape, BF16),
            pltpu.VMEM(wstep.shape, BF16),
            pltpu.VMEM(wbc.shape, BF16),
            pltpu.VMEM((rows * tokens, depth), BF16),
            pltpu.VMEM((rows * tokens, out_width), BF16),
            pltpu.VMEM((rows, tokens, out_width), BF16),
            pltpu.VMEM((rows, tokens, out_width), BF16),
            pltpu.VMEM((heads, tokens, 128), F32),
            dma((4,)),
            dma((pieces,)),
            dma((rows * share,)),
            dma((heads, rows)),
            dma((heads, rows)),
            dma((heads,)),
            dma((heads,)),
            dma((rows, n_chunks)),
            dma((rows, n_chunks)),
            dma((rows, n_chunks)),
        ],
        compiler_params=pltpu.CompilerParams(
            collective_id=0, has_side_effects=True, vmem_limit_bytes=LIMIT
        ),
        name="project",
    )(scaled, stats, wsig, wgate, wstep, wbc)


def scan_kernel(
    positions, index_ref, live_ref, proj_ref, low_ref, bias_ref, rate_ref, skip_ref, gain_ref,
    spread_ref, state_ref, *rest
):
    ups, (new_ref, gated_ref, sq_ref) = rest[:GROUP], rest[GROUP:]
    g = pl.program_id(0)
    rows = proj_ref.shape[0]
    inner = ups[0].shape[2]
    rank = ups[0].shape[1]
    n_state = state_ref.shape[3]
    shape_state = state_ref.shape[1:]
    base = 2 * inner
    xin = proj_ref[:, :inner]
    zin = proj_ref[:, inner:base]
    bc = proj_ref[:, base : base + 2 * n_state]
    dtin = proj_ref[:, base + 2 * n_state :]
    low = low_ref[:, : GROUP * rank].astype(BF16)
    up = jnp.concatenate([u[0] for u in ups], axis=0)
    x = jax.nn.silu(xin + jnp.dot(low, up, preferred_element_type=F32))
    bgate = jax.nn.silu(bc[:, :n_state])
    cgate = jax.nn.silu(bc[:, n_state:])
    row1 = lax.broadcasted_iota(jnp.int32, (rows, 1), 0)
    stream1 = row1 // positions
    live = (g * GROUP + stream1) < live_ref[0]

    def padded(ref):
        blank = jnp.zeros((1, dtin.shape[1] - ref.shape[1]), F32)
        return jnp.concatenate([ref[...], blank], axis=1)

    dt = jax.nn.softplus(dtin + padded(bias_ref))
    decay = jnp.exp(-dt * padded(rate_ref))
    sk_high, sk_low = split2(jnp.broadcast_to(padded(skip_ref), dt.shape))
    dt_high, dt_low = split2(dt)
    de_high, de_low = split2(decay)
    spread = jnp.dot(
        jnp.concatenate([dt_high, dt_low, de_high, de_low, sk_high, sk_low], axis=0), spread_ref[...],
        preferred_element_type=F32,
    )
    dt_wide = spread[:rows] + spread[rows : 2 * rows]
    de_wide = spread[2 * rows : 3 * rows] + spread[3 * rows : 4 * rows]
    u = jnp.where(live, dt_wide * x, 0.0)
    de_wide = jnp.where(live, de_wide, 1.0)

    second = lax.rem(row1, positions) == 1
    prev_de = pltpu.roll(de_wide, 1, 0)
    prev_u = pltpu.roll(u, 1, 0)
    prev_b = pltpu.roll(bgate, 1, 0)
    keep = jnp.where(second, de_wide * prev_de, de_wide)
    carried_u = jnp.where(second, u, u * pltpu.roll(de_wide, rows - 1, 0))
    keep_high, keep_low = split2(keep)
    left = jnp.concatenate(
        [carried_u.astype(BF16), keep_high, keep_low, jnp.zeros_like(keep_low)], axis=0
    )
    left = left.T
    y = jnp.zeros((rows, inner), F32)
    zero_b = jnp.zeros((rows, n_state), F32)
    for j in range(GROUP):
        mine = stream1 == j
        b_mine = jnp.where(mine, bgate, 0.0)
        ones_mine = jnp.broadcast_to(jnp.where(mine & second, 1.0, 0.0), (rows, n_state))
        right = jnp.concatenate(
            [
                jnp.concatenate([b_mine, zero_b], axis=1),
                jnp.concatenate([zero_b, ones_mine], axis=1),
                jnp.concatenate([zero_b, ones_mine], axis=1),
                jnp.concatenate([zero_b, zero_b], axis=1),
            ],
            axis=0,
        ).astype(BF16)
        state = state_ref[j].reshape(inner, n_state)
        both = jnp.dot(left, right, preferred_element_type=F32)
        new = state.astype(F32) * both[:, n_state:] + both[:, :n_state]
        new_ref[j] = new.astype(BF16).reshape(shape_state)
        y = y + nt(jnp.where(mine, cgate, 0.0).astype(BF16), state)

    dot_own = jnp.sum(bgate * cgate, -1, keepdims=True)
    dot_prev = jnp.sum(prev_b * cgate, -1, keepdims=True)
    y = keep * y + u * dot_own + jnp.where(second, de_wide * prev_u * dot_prev, 0.0)
    y = y + (spread[4 * rows : 5 * rows] + spread[5 * rows :]) * x
    gated = y * jax.nn.silu(zin)
    gated_ref[...] = (gated * gain_ref[...]).astype(BF16)
    sq_ref[...] = jnp.broadcast_to(jnp.sum(gated * gated, -1, keepdims=True), sq_ref.shape)


def scan(index, live, proj, low, bias, rate, skip, gain, state, up, positions):
    tokens, out_width = proj.shape
    capacity, rank, inner = up.shape
    rows = GROUP * positions
    heads_here = bias.shape[0]
    head_size = inner // heads_here
    spread = (jnp.arange(128)[:, None] == jnp.arange(inner)[None, :] // head_size).astype(BF16)
    bias, rate, skip = bias.reshape(1, -1), rate.reshape(1, -1), skip.reshape(1, -1)

    def up_spec(j):
        return pl.BlockSpec(
            (1, rank, inner), lambda g, idx, lv: (lax.rem(idx[g * GROUP + j], capacity), 0, 0)
        )

    def whole(a):
        return pl.BlockSpec(a.shape, lambda g, idx, lv: (0, 0))

    def by_rows(w):
        return pl.BlockSpec((rows, w), lambda g, idx, lv: (g, 0))

    gain = gain.reshape(1, -1)
    state_spec = pl.BlockSpec((GROUP,) + state.shape[1:], lambda g, idx, lv: (g, 0, 0, 0))
    return pl.pallas_call(
        functools.partial(scan_kernel, positions),
        grid_spec=pltpu.PrefetchScalarGridSpec(
            num_scalar_prefetch=2,
            grid=(tokens // rows,),
            in_specs=[by_rows(out_width), by_rows(128), whole(bias), whole(rate), whole(skip),
                      whole(gain), whole(spread), state_spec]
            + [up_spec(j) for j in range(GROUP)],
            out_specs=[state_spec, by_rows(inner), by_rows(128)],
        ),
        out_shape=[
            jax.ShapeDtypeStruct(state.shape, BF16),
            jax.ShapeDtypeStruct((tokens, inner), BF16),
            jax.ShapeDtypeStruct((tokens, 128), F32),
        ],
        compiler_params=pltpu.CompilerParams(vmem_limit_bytes=LIMIT),
        name="scan",
    )(index, live, proj, low, bias, rate, skip, gain, spread, state, *([up] * GROUP))


def output_kernel(
    heads, positions, inner_width, live_ref, gated_ref, sq_ref, hidden_ref, w_ref, out_ref,
    wbuf, pbuf, rbuf, sbuf, w_sem, send_s, recv_s, send_r, recv_r,
):
    h = lax.axis_index("head")
    tokens, width = hidden_ref.shape
    order = [d for d in range(1, heads)] + [0]
    order = sorted(order, key=lambda d: (d == 0, abs(d - heads // 2)))

    def load(d):
        to = lax.rem(h + d, heads)
        return pltpu.make_async_copy(
            w_ref.at[:, pl.ds(pl.multiple_of(to * width, 128), width)], wbuf.at[d], w_sem.at[d]
        )

    for d in order:
        load(d).start()
    barrier = pltpu.get_barrier_semaphore()
    for d in range(1, heads):
        pl.semaphore_signal(
            barrier, inc=1, device_id={"head": lax.rem(h + d, heads)}, device_id_type=MESH
        )
    pl.semaphore_wait(barrier, heads - 1)
    copies = []
    for d in range(1, heads):
        copy = pltpu.make_async_remote_copy(
            src_ref=sq_ref, dst_ref=sbuf.at[d], send_sem=send_s.at[d], recv_sem=recv_s.at[d],
            device_id={"head": lax.rem(h + d, heads)}, device_id_type=MESH,
        )
        copy.start()
        copies.append(copy)
    parts = {}
    step = min(width, 512)
    for d in order:
        load(d).wait()
        for c in range(0, width, step):
            pbuf[d, :, c : c + step] = jnp.dot(
                gated_ref[...], wbuf[d, :, c : c + step], preferred_element_type=F32
            ).astype(BF16)
        if d:
            copy = pltpu.make_async_remote_copy(
                src_ref=pbuf.at[d], dst_ref=rbuf.at[d], send_sem=send_r.at[d],
                recv_sem=recv_r.at[d],
                device_id={"head": lax.rem(h + d, heads)}, device_id_type=MESH,
            )
            copy.start()
            parts[d] = copy
    square = sq_ref[...]
    for d in range(1, heads):
        copies[d - 1].wait_recv()
        square = square + sbuf[d]
    inverse = lax.rsqrt(square[:, :1] / inner_width + EPSILON)
    mixer = pbuf[0].astype(F32)
    for d in sorted(parts, key=lambda d: -abs(d - heads // 2)):
        parts[d].wait_recv()
        mixer = mixer + rbuf[d].astype(F32)
    stream = lax.broadcasted_iota(jnp.int32, (tokens, 1), 0) // positions
    live = stream < live_ref[0]
    out_ref[...] = (
        hidden_ref[...].astype(F32) + jnp.where(live, mixer * inverse, 0.0)
    ).astype(BF16)
    for copy in copies:
        copy.wait_send()
    for copy in parts.values():
        copy.wait_send()


def output(live, gated, sq, hidden, weight, heads, positions):
    tokens, width = hidden.shape
    inner = gated.shape[1]
    dma = pltpu.SemaphoreType.DMA
    return pl.pallas_call(
        functools.partial(output_kernel, heads, positions, float(inner * heads)),
        out_shape=jax.ShapeDtypeStruct((tokens, width), BF16),
        in_specs=[SM, VM, VM, VM, ANY],
        out_specs=VM,
        scratch_shapes=[
            pltpu.VMEM((heads, inner, width), BF16),
            pltpu.VMEM((heads, tokens, width), BF16),
            pltpu.VMEM((heads, tokens, width), BF16),
            pltpu.VMEM((heads, tokens, 128), F32),
            dma((heads,)),
            dma((heads,)),
            dma((heads,)),
            dma((heads,)),
            dma((heads,)),
        ],
        compiler_params=pltpu.CompilerParams(
            collective_id=1, has_side_effects=True, vmem_limit_bytes=LIMIT
        ),
        name="output",
    )(live, gated, sq, hidden, weight)


def on_device(
    heads, rows,
    hidden, input_norm_scale, projection_signal, projection_gate, projection_step,
    projection_input_output, step_bias, head_decay_rate, head_skip_weight, gated_norm_scale,
    adapter_down_weight, adapter_up_weight, output_weight, scan_state, stream_tenant_index,
    live_block_rows,
):
    streams, positions, width = hidden.shape
    flat = hidden.reshape(streams * positions, width)
    down = jnp.swapaxes(adapter_down_weight, 1, 2)
    scaled, stats = front(flat, input_norm_scale, down, stream_tenant_index, positions)
    proj, low = project(
        scaled, stats, projection_signal, projection_gate, projection_step.T,
        projection_input_output, heads, rows,
    )
    new_state, gated, sq = scan(
        stream_tenant_index, live_block_rows, proj, low, step_bias, head_decay_rate,
        head_skip_weight, gated_norm_scale, scan_state, adapter_up_weight, positions,
    )
    mixed = output(live_block_rows, gated, sq, flat, output_weight, heads, positions)
    return mixed.reshape(hidden.shape), new_state


def solution(mesh):
    in_specs = (
        P(("rep", "row"), None, "head"),
        P("head"),
        P("row", "head"),
        P("row", "head"),
        P("row", "head"),
        P("row", None),
        P("head"),
        P("head"),
        P("head"),
        P("head"),
        P("row", "head", None),
        P("row", None, "head"),
        P("head", None),
        P(("rep", "row"), "head", None, None),
        P(("rep", "row")),
        P(("rep", "row")),
    )
    out_specs = (P(("rep", "row"), None, "head"), P(("rep", "row"), "head", None, None))
    return jax.shard_map(
        functools.partial(on_device, mesh.shape["head"], mesh.shape["row"]),
        mesh=mesh, in_specs=in_specs, out_specs=out_specs, check_vma=False,
    )
```

```python
import functools

import jax
import jax.numpy as jnp
from jax import lax
from jax.experimental import pallas as pl
from jax.experimental.pallas import tpu as pltpu
from jax.sharding import PartitionSpec as P

EPSILON = 1e-05
GROUP = 4
BF16 = jnp.bfloat16
F32 = jnp.float32
MESH = pl.DeviceIdType.MESH
LIMIT = 48 * 1024 * 1024
ANY = pl.BlockSpec(memory_space=pl.ANY)
VM = pl.BlockSpec(memory_space=pltpu.VMEM)
SM = pl.BlockSpec(memory_space=pltpu.SMEM)


def nt(a, b):
    return lax.dot_general(a, b, (((1,), (1,)), ((), ())), preferred_element_type=F32)


def split2(a):
    high = a.astype(BF16)
    return high, (a - high.astype(F32)).astype(BF16)


def front_kernel(
    capacity, positions, index_ref, hidden_ref, scale_ref, down_ref, scaled_ref, stats_ref,
    dbuf, sems,
):
    tokens = hidden_ref.shape[0]
    rank = down_ref.shape[1]
    copies = []
    for s in range(tokens // positions):
        copy = pltpu.make_async_copy(
            down_ref.at[lax.rem(index_ref[s], capacity)],
            dbuf.at[s * rank : (s + 1) * rank, :], sems.at[s],
        )
        copy.start()
        copies.append(copy)
    wide = hidden_ref[...].astype(F32)
    scaled_ref[...] = (wide * scale_ref[...]).astype(BF16)
    squares = jnp.sum(wide * wide, -1, keepdims=True)
    streams = 2 * GROUP
    rows = streams * positions
    lanes = streams * rank
    row = lax.broadcasted_iota(jnp.int32, (rows, lanes), 0) // positions
    col = lax.broadcasted_iota(jnp.int32, (rows, lanes), 1) // rank
    for g in range(tokens // rows):
        for copy in copies[g * streams : (g + 1) * streams]:
            copy.wait()
        here = slice(g * rows, (g + 1) * rows)
        low = nt(scaled_ref[here, :], dbuf[g * lanes : (g + 1) * lanes, :])
        low = jnp.where(row < GROUP, low, pltpu.roll(low, lanes // 2, 1))
        low = jnp.where(lax.rem(row, GROUP) == col, low, 0.0)
        stats_ref[here, :] = jnp.where(col < GROUP, low, squares[here, :])


def front(hidden, scale, down, index, positions):
    tokens, width = hidden.shape
    capacity, rank, _ = down.shape
    streams = tokens // positions
    return pl.pallas_call(
        functools.partial(front_kernel, capacity, positions),
        in_specs=[SM, VM, VM, ANY],
        out_specs=[VM, VM],
        out_shape=[
            jax.ShapeDtypeStruct((tokens, width), BF16),
            jax.ShapeDtypeStruct((tokens, 128), F32),
        ],
        scratch_shapes=[
            pltpu.VMEM((streams * rank, width), BF16),
            pltpu.SemaphoreType.DMA((streams,)),
        ],
        compiler_params=pltpu.CompilerParams(vmem_limit_bytes=57 * 1024 * 1024),
        name="front",
    )(index, hidden, scale.reshape(1, -1), down)


def project_kernel(
    heads, rows, model_width, scaled_ref, stats_ref, wsig_ref, wgate_ref, wstep_ref, wbc_ref,
    proj_ref, low_ref,
    wsig, wgate, wstep, wbc, xbuf, pbuf, rup, rdown, sbuf,
    w_sem, send_a, recv_a, send_b, recv_b, send_f, recv_f, send_s, recv_s, send_r, recv_u, recv_d,
):
    h = lax.axis_index("head")
    r = lax.axis_index("row")
    tokens, width = scaled_ref.shape
    share = heads // rows
    pieces = min(heads, tokens // 16)
    every = heads // pieces
    prow = tokens // pieces
    inner = wsig.shape[1]
    heads_here = wstep.shape[0]
    loads = [
        pltpu.make_async_copy(s, d, w_sem.at[i])
        for i, (s, d) in enumerate(
            [(wbc_ref, wbc), (wstep_ref, wstep), (wsig_ref, wsig), (wgate_ref, wgate)]
        )
    ]
    for load in loads:
        load.start()
    target_row = h // share
    piece = h // every

    def when(condition):
        return (lambda f: f()) if condition is True else pl.when(condition)

    is_owner = True if every == 1 else (lax.rem(h, every) == 0)

    barrier = pltpu.get_barrier_semaphore()
    for d in range(1, heads):
        pl.semaphore_signal(
            barrier, inc=1, device_id={"head": lax.rem(h + d, heads)}, device_id_type=MESH
        )
    for d in range(1, rows):
        pl.semaphore_signal(
            barrier, inc=1, device_id={"row": lax.rem(r + d, rows)}, device_id_type=MESH
        )

    @when(is_owner)
    def _():
        for j in range(share):
            for e in range(rows):
                src_h = r * share + j
                src_r = lax.rem(r + e, rows)
                same = jnp.logical_and(src_h == h, src_r == r)

                @pl.when(jnp.logical_not(same))
                def _():
                    pl.semaphore_signal(
                        barrier, inc=1, device_id={"head": src_h, "row": src_r},
                        device_id_type=MESH,
                    )

    to_self = jnp.logical_and(lax.rem(h, every) == 0, target_row == r).astype(jnp.int32)
    pl.semaphore_wait(barrier, heads - 1 + rows - 1 + pieces - to_self)

    def a_parts(k):
        src = scaled_ref.at[pl.ds(k * prow, prow), :]
        row0 = pl.multiple_of(r * tokens + k * prow, 16)
        col0 = pl.multiple_of(lax.rem(h, share) * width, 128)
        return src, xbuf.at[pl.ds(row0, prow), pl.ds(col0, width)]

    def a_remote(k):
        src, dst = a_parts(k)
        return pltpu.make_async_remote_copy(
            src_ref=src, dst_ref=dst, send_sem=send_a.at[k],
            recv_sem=recv_a.at[r * share + lax.rem(h, share)],
            device_id={"head": k * every, "row": target_row}, device_id_type=MESH,
        )

    def a_same(k):
        return jnp.logical_and(h == k * every, target_row == r)

    for k in range(pieces):
        @pl.when(jnp.logical_not(a_same(k)))
        def _():
            a_remote(k).start()

        @pl.when(a_same(k))
        def _():
            src, dst = a_parts(k)
            pltpu.make_async_copy(src, dst, recv_a.at[r * share + lax.rem(h, share)]).start()

    stat_copies = []
    for d in range(1, heads):
        copy = pltpu.make_async_remote_copy(
            src_ref=stats_ref, dst_ref=sbuf.at[d], send_sem=send_s.at[d], recv_sem=recv_s.at[d],
            device_id={"head": lax.rem(h + d, heads)}, device_id_type=MESH,
        )
        copy.start()
        stat_copies.append(copy)

    pbuf[:, 2 * inner + wbc.shape[1] :] = jnp.zeros((rows * tokens, 128), BF16)

    def block_rows(e, k):
        row0 = lax.rem(r + e, rows) * tokens + k * prow
        return xbuf.at[pl.ds(pl.multiple_of(row0, 16), prow), :]

    chips = heads // 2
    chip, core = h // 2, lax.rem(h, 2)
    partner = chip * 2 + 1 - core

    def owns(head):
        return True if every == 1 else lax.rem(head, every) == 0

    def b_copy(dx, e, k):
        to = lax.rem(chip + dx, chips) * 2 + core if dx else partner
        return pltpu.make_async_remote_copy(
            src_ref=block_rows(e, k), dst_ref=block_rows(e, k),
            send_sem=send_b.at[dx, e], recv_sem=recv_b.at[dx, e],
            device_id={"head": to}, device_id_type=MESH,
        )

    def origin(dx, its_core):
        return lax.rem(chip - dx + chips, chips) * 2 + its_core

    def f_copy(dx, e, its_core):
        block = block_rows(e, origin(dx, its_core) // every)
        return pltpu.make_async_remote_copy(
            src_ref=block, dst_ref=block,
            send_sem=send_f.at[dx, e], recv_sem=recv_f.at[dx, e],
            device_id={"head": partner}, device_id_type=MESH,
        )

    @when(is_owner)
    def _():
        for e in range(rows):
            src_r = lax.rem(r + e, rows)
            for j in range(share):
                dst = xbuf.at[
                    pl.ds(pl.multiple_of(src_r * tokens + piece * prow, 16), prow),
                    pl.ds(j * width, width),
                ]
                pltpu.make_async_copy(dst, dst, recv_a.at[src_r * share + j]).wait()
            for dx in list(range(1, chips)) + [0]:
                b_copy(dx, e, piece).start()

    for e in range(rows):
        for dx in range(1, chips):
            @when(owns(origin(dx, core)))
            def _():
                b_copy(dx, e, origin(dx, core) // every).wait_recv()
                f_copy(dx, e, core).start()

    for e in range(rows):
        @when(owns(partner))
        def _():
            b_copy(0, e, partner // every).wait_recv()

        for dx in range(1, chips):
            @when(owns(origin(dx, 1 - core)))
            def _():
                f_copy(dx, e, 1 - core).wait_recv()

    bc_width = wbc.shape[1]
    half = min(inner, 512)
    chunks = [(wbc, 0, bc_width, 2 * inner, 0), (wstep, None, 128, 2 * inner + bc_width, 1)]
    for i, w in ((2, wsig), (3, wgate)):
        for c in range(0, inner, half):
            chunks.append((w, c, half, (i - 2) * inner + c, i))

    def columns(n):
        return slice(chunks[n][3], chunks[n][3] + chunks[n][2])

    def hop(t, n, up):
        there = lax.rem(r + (1 if up else rows - 1), rows)
        return pltpu.make_async_remote_copy(
            src_ref=pbuf.at[t * tokens : (t + 1) * tokens, columns(n)],
            dst_ref=(rup if up else rdown).at[t, :, columns(n)],
            send_sem=send_r.at[t, n], recv_sem=(recv_u if up else recv_d).at[t, n],
            device_id={"row": there}, device_id_type=MESH,
        )

    def first_hop(n):
        @pl.when(r == 0)
        def _():
            for t in range(rows - 1, 0, -1):
                hop(t, n, True).start()

        @pl.when(r == rows - 1)
        def _():
            for t in range(rows - 1):
                hop(t, n, False).start()

    def pass_on(t, n, up):
        copy = hop(t, n, up)
        copy.wait_recv()
        here = slice(t * tokens, (t + 1) * tokens)
        came = (rup if up else rdown)[t, :, columns(n)]
        pbuf[here, columns(n)] = (
            pbuf[here, columns(n)].astype(F32) + came.astype(F32)
        ).astype(BF16)
        copy.start()

    waited = set()
    for n, (w, c, cw, out, load) in enumerate(chunks):
        if load not in waited:
            loads[load].wait()
            waited.add(load)
        if c is None:
            pbuf[:, out : out + heads_here] = nt(xbuf[...], w[...]).astype(BF16)
        else:
            pbuf[:, out : out + cw] = jnp.dot(
                xbuf[...], w[:, c : c + cw], preferred_element_type=F32
            ).astype(BF16)
        first_hop(n)

    for step in range(len(chunks) + rows - 3):
        for k in range(1, rows - 1):
            n = step - (k - 1)
            if 0 <= n < len(chunks):
                @pl.when(r == k)
                def _():
                    for t in range(rows - 1, k, -1):
                        pass_on(t, n, True)

                @pl.when(r == rows - 1 - k)
                def _():
                    for t in range(rows - 1 - k):
                        pass_on(t, n, False)

    total = stats_ref[...]
    for d in range(1, heads):
        stat_copies[d - 1].wait_recv()
        total = total + sbuf[d]
    inverse = lax.rsqrt(total[:, 127:128] / model_width + EPSILON)
    low_ref[...] = total * inverse
    own = pl.ds(pl.multiple_of(r * tokens, 16), tokens)
    for n in range(len(chunks)):
        proj_ref[:, columns(n)] = pbuf[own, columns(n)].astype(F32)
        for buffer, sem, there in ((rup, recv_u, r > 0), (rdown, recv_d, r < rows - 1)):
            @pl.when(there)
            def _():
                came = buffer.at[r, :, columns(n)]
                pltpu.make_async_copy(came, came, sem.at[r, n]).wait()
                proj_ref[:, columns(n)] = proj_ref[:, columns(n)] + came[...].astype(F32)
        proj_ref[:, columns(n)] = proj_ref[:, columns(n)] * inverse

    for n in range(len(chunks)):
        for t in range(rows):
            @pl.when(t > r)
            def _():
                hop(t, n, True).wait_send()

            @pl.when(t < r)
            def _():
                hop(t, n, False).wait_send()
    for copy in stat_copies:
        copy.wait_send()
    for k in range(pieces):
        @pl.when(jnp.logical_not(a_same(k)))
        def _():
            a_remote(k).wait_send()

    @when(is_owner)
    def _():
        for e in range(rows):
            for dx in range(chips):
                b_copy(dx, e, piece).wait_send()

    for e in range(rows):
        for dx in range(1, chips):
            @when(owns(origin(dx, core)))
            def _():
                f_copy(dx, e, core).wait_send()


def project(scaled, stats, wsig, wgate, wstep, wbc, heads, rows):
    tokens, width = scaled.shape
    depth, inner = wsig.shape
    out_width = 2 * inner + wbc.shape[1] + 128
    share = heads // rows
    pieces = min(heads, tokens // 16)
    n_chunks = 2 + 2 * (inner // min(inner, 512))
    dma = pltpu.SemaphoreType.DMA
    return pl.pallas_call(
        functools.partial(project_kernel, heads, rows, float(width * heads)),
        out_shape=[
            jax.ShapeDtypeStruct((tokens, out_width), F32),
            jax.ShapeDtypeStruct((tokens, 128), F32),
        ],
        in_specs=[VM, VM, ANY, ANY, ANY, ANY],
        out_specs=[VM, VM],
        scratch_shapes=[
            pltpu.VMEM(wsig.shape, BF16),
            pltpu.VMEM(wgate.shape, BF16),
            pltpu.VMEM(wstep.shape, BF16),
            pltpu.VMEM(wbc.shape, BF16),
            pltpu.VMEM((rows * tokens, depth), BF16),
            pltpu.VMEM((rows * tokens, out_width), BF16),
            pltpu.VMEM((rows, tokens, out_width), BF16),
            pltpu.VMEM((rows, tokens, out_width), BF16),
            pltpu.VMEM((heads, tokens, 128), F32),
            dma((4,)),
            dma((pieces,)),
            dma((rows * share,)),
            dma((heads // 2, rows)),
            dma((heads // 2, rows)),
            dma((heads // 2, rows)),
            dma((heads // 2, rows)),
            dma((heads,)),
            dma((heads,)),
            dma((rows, n_chunks)),
            dma((rows, n_chunks)),
            dma((rows, n_chunks)),
        ],
        compiler_params=pltpu.CompilerParams(
            collective_id=0, has_side_effects=True, vmem_limit_bytes=LIMIT
        ),
        name="project",
    )(scaled, stats, wsig, wgate, wstep, wbc)


def scan_kernel(
    positions, index_ref, live_ref, proj_ref, low_ref, bias_ref, rate_ref, skip_ref, gain_ref,
    spread_ref, state_ref, *rest
):
    ups, (new_ref, gated_ref, sq_ref) = rest[:GROUP], rest[GROUP:]
    g = pl.program_id(0)
    rows = proj_ref.shape[0]
    inner = ups[0].shape[2]
    rank = ups[0].shape[1]
    n_state = state_ref.shape[3]
    shape_state = state_ref.shape[1:]
    base = 2 * inner
    xin = proj_ref[:, :inner]
    zin = proj_ref[:, inner:base]
    bc = proj_ref[:, base : base + 2 * n_state]
    dtin = proj_ref[:, base + 2 * n_state :]
    low = low_ref[:, : GROUP * rank].astype(BF16)
    up = jnp.concatenate([u[0] for u in ups], axis=0)
    x = jax.nn.silu(xin + jnp.dot(low, up, preferred_element_type=F32))
    bgate = jax.nn.silu(bc[:, :n_state])
    cgate = jax.nn.silu(bc[:, n_state:])
    row1 = lax.broadcasted_iota(jnp.int32, (rows, 1), 0)
    stream1 = row1 // positions
    live = (g * GROUP + stream1) < live_ref[0]

    def padded(ref):
        blank = jnp.zeros((1, dtin.shape[1] - ref.shape[1]), F32)
        return jnp.concatenate([ref[...], blank], axis=1)

    dt = jax.nn.softplus(dtin + padded(bias_ref))
    decay = jnp.exp(-dt * padded(rate_ref))
    sk_high, sk_low = split2(jnp.broadcast_to(padded(skip_ref), dt.shape))
    dt_high, dt_low = split2(dt)
    de_high, de_low = split2(decay)
    spread = jnp.dot(
        jnp.concatenate([dt_high, dt_low, de_high, de_low, sk_high, sk_low], axis=0), spread_ref[...],
        preferred_element_type=F32,
    )
    dt_wide = spread[:rows] + spread[rows : 2 * rows]
    de_wide = spread[2 * rows : 3 * rows] + spread[3 * rows : 4 * rows]
    u = jnp.where(live, dt_wide * x, 0.0)
    de_wide = jnp.where(live, de_wide, 1.0)

    second = lax.rem(row1, positions) == 1
    prev_de = pltpu.roll(de_wide, 1, 0)
    prev_u = pltpu.roll(u, 1, 0)
    prev_b = pltpu.roll(bgate, 1, 0)
    keep = jnp.where(second, de_wide * prev_de, de_wide)
    carried_u = jnp.where(second, u, u * pltpu.roll(de_wide, rows - 1, 0))
    keep_high, keep_low = split2(keep)
    left = jnp.concatenate(
        [carried_u.astype(BF16), keep_high, keep_low, jnp.zeros_like(keep_low)], axis=0
    )
    left = left.T
    y = jnp.zeros((rows, inner), F32)
    zero_b = jnp.zeros((rows, n_state), F32)
    for j in range(GROUP):
        mine = stream1 == j
        b_mine = jnp.where(mine, bgate, 0.0)
        ones_mine = jnp.broadcast_to(jnp.where(mine & second, 1.0, 0.0), (rows, n_state))
        right = jnp.concatenate(
            [
                jnp.concatenate([b_mine, zero_b], axis=1),
                jnp.concatenate([zero_b, ones_mine], axis=1),
                jnp.concatenate([zero_b, ones_mine], axis=1),
                jnp.concatenate([zero_b, zero_b], axis=1),
            ],
            axis=0,
        ).astype(BF16)
        state = state_ref[j].reshape(inner, n_state)
        both = jnp.dot(left, right, preferred_element_type=F32)
        new = state.astype(F32) * both[:, n_state:] + both[:, :n_state]
        new_ref[j] = new.astype(BF16).reshape(shape_state)
        y = y + nt(jnp.where(mine, cgate, 0.0).astype(BF16), state)

    dot_own = jnp.sum(bgate * cgate, -1, keepdims=True)
    dot_prev = jnp.sum(prev_b * cgate, -1, keepdims=True)
    y = keep * y + u * dot_own + jnp.where(second, de_wide * prev_u * dot_prev, 0.0)
    y = y + (spread[4 * rows : 5 * rows] + spread[5 * rows :]) * x
    gated = y * jax.nn.silu(zin)
    gated_ref[...] = (gated * gain_ref[...]).astype(BF16)
    sq_ref[...] = jnp.broadcast_to(jnp.sum(gated * gated, -1, keepdims=True), sq_ref.shape)


def scan(index, live, proj, low, bias, rate, skip, gain, state, up, positions):
    tokens, out_width = proj.shape
    capacity, rank, inner = up.shape
    rows = GROUP * positions
    heads_here = bias.shape[0]
    head_size = inner // heads_here
    spread = (jnp.arange(128)[:, None] == jnp.arange(inner)[None, :] // head_size).astype(BF16)
    bias, rate, skip = bias.reshape(1, -1), rate.reshape(1, -1), skip.reshape(1, -1)

    def up_spec(j):
        return pl.BlockSpec(
            (1, rank, inner), lambda g, idx, lv: (lax.rem(idx[g * GROUP + j], capacity), 0, 0)
        )

    def whole(a):
        return pl.BlockSpec(a.shape, lambda g, idx, lv: (0, 0))

    def by_rows(w):
        return pl.BlockSpec((rows, w), lambda g, idx, lv: (g, 0))

    gain = gain.reshape(1, -1)
    state_spec = pl.BlockSpec((GROUP,) + state.shape[1:], lambda g, idx, lv: (g, 0, 0, 0))
    return pl.pallas_call(
        functools.partial(scan_kernel, positions),
        grid_spec=pltpu.PrefetchScalarGridSpec(
            num_scalar_prefetch=2,
            grid=(tokens // rows,),
            in_specs=[by_rows(out_width), by_rows(128), whole(bias), whole(rate), whole(skip),
                      whole(gain), whole(spread), state_spec]
            + [up_spec(j) for j in range(GROUP)],
            out_specs=[state_spec, by_rows(inner), by_rows(128)],
        ),
        out_shape=[
            jax.ShapeDtypeStruct(state.shape, BF16),
            jax.ShapeDtypeStruct((tokens, inner), BF16),
            jax.ShapeDtypeStruct((tokens, 128), F32),
        ],
        compiler_params=pltpu.CompilerParams(vmem_limit_bytes=LIMIT),
        name="scan",
    )(index, live, proj, low, bias, rate, skip, gain, spread, state, *([up] * GROUP))


def output_kernel(
    heads, positions, inner_width, live_ref, gated_ref, sq_ref, hidden_ref, w_ref, out_ref,
    wbuf, pbuf, rbuf, sbuf, w_sem, send_s, recv_s, send_r, recv_r,
):
    h = lax.axis_index("head")
    tokens, width = hidden_ref.shape
    chips = heads // 2
    chip, core = h // 2, lax.rem(h, 2)
    partner = chip * 2 + 1 - core
    order = [2 * dx + k for dx in list(range(1, chips)) + [0] for k in range(2)]

    def target(d):
        its_core = core if d % 2 else 1 - core
        return lax.rem(chip + d // 2, chips) * 2 + its_core

    def load(d):
        to = target(d)
        return pltpu.make_async_copy(
            w_ref.at[:, pl.ds(pl.multiple_of(to * width, 128), width)], wbuf.at[d], w_sem.at[d]
        )

    for d in order:
        load(d).start()
    barrier = pltpu.get_barrier_semaphore()
    for d in range(1, heads):
        pl.semaphore_signal(
            barrier, inc=1, device_id={"head": lax.rem(h + d, heads)}, device_id_type=MESH
        )
    pl.semaphore_wait(barrier, heads - 1)
    copies = []
    for d in range(1, heads):
        copy = pltpu.make_async_remote_copy(
            src_ref=sq_ref, dst_ref=sbuf.at[d], send_sem=send_s.at[d], recv_sem=recv_s.at[d],
            device_id={"head": lax.rem(h + d, heads)}, device_id_type=MESH,
        )
        copy.start()
        copies.append(copy)
    parts = {}
    step = min(width, 512)
    for d in order:
        load(d).wait()
        for c in range(0, width, step):
            pbuf[d, :, c : c + step] = jnp.dot(
                gated_ref[...], wbuf[d, :, c : c + step], preferred_element_type=F32
            ).astype(BF16)
        if d == 1:
            continue
        if d % 2:
            parts[d - 1].wait_recv()
            pbuf[d] = (pbuf[d].astype(F32) + rbuf[d - 1].astype(F32)).astype(BF16)
        copy = pltpu.make_async_remote_copy(
            src_ref=pbuf.at[d], dst_ref=rbuf.at[d], send_sem=send_r.at[d],
            recv_sem=recv_r.at[d],
            device_id={"head": target(d) if d % 2 else partner}, device_id_type=MESH,
        )
        copy.start()
        parts[d] = copy
    square = sq_ref[...]
    for d in range(1, heads):
        copies[d - 1].wait_recv()
        square = square + sbuf[d]
    inverse = lax.rsqrt(square[:, :1] / inner_width + EPSILON)
    mixer = pbuf[1].astype(F32)
    for d in [0] + [2 * dx + 1 for dx in range(1, chips)]:
        parts[d].wait_recv()
        mixer = mixer + rbuf[d].astype(F32)
    stream = lax.broadcasted_iota(jnp.int32, (tokens, 1), 0) // positions
    live = stream < live_ref[0]
    out_ref[...] = (
        hidden_ref[...].astype(F32) + jnp.where(live, mixer * inverse, 0.0)
    ).astype(BF16)
    for copy in copies:
        copy.wait_send()
    for copy in parts.values():
        copy.wait_send()


def output(live, gated, sq, hidden, weight, heads, positions):
    tokens, width = hidden.shape
    inner = gated.shape[1]
    dma = pltpu.SemaphoreType.DMA
    return pl.pallas_call(
        functools.partial(output_kernel, heads, positions, float(inner * heads)),
        out_shape=jax.ShapeDtypeStruct((tokens, width), BF16),
        in_specs=[SM, VM, VM, VM, ANY],
        out_specs=VM,
        scratch_shapes=[
            pltpu.VMEM((heads, inner, width), BF16),
            pltpu.VMEM((heads, tokens, width), BF16),
            pltpu.VMEM((heads, tokens, width), BF16),
            pltpu.VMEM((heads, tokens, 128), F32),
            dma((heads,)),
            dma((heads,)),
            dma((heads,)),
            dma((heads,)),
            dma((heads,)),
        ],
        compiler_params=pltpu.CompilerParams(
            collective_id=1, has_side_effects=True, vmem_limit_bytes=LIMIT
        ),
        name="output",
    )(live, gated, sq, hidden, weight)


def on_device(
    heads, rows,
    hidden, input_norm_scale, projection_signal, projection_gate, projection_step,
    projection_input_output, step_bias, head_decay_rate, head_skip_weight, gated_norm_scale,
    adapter_down_weight, adapter_up_weight, output_weight, scan_state, stream_tenant_index,
    live_block_rows,
):
    streams, positions, width = hidden.shape
    flat = hidden.reshape(streams * positions, width)
    down = jnp.swapaxes(adapter_down_weight, 1, 2)
    scaled, stats = front(flat, input_norm_scale, down, stream_tenant_index, positions)
    proj, low = project(
        scaled, stats, projection_signal, projection_gate, projection_step.T,
        projection_input_output, heads, rows,
    )
    new_state, gated, sq = scan(
        stream_tenant_index, live_block_rows, proj, low, step_bias, head_decay_rate,
        head_skip_weight, gated_norm_scale, scan_state, adapter_up_weight, positions,
    )
    mixed = output(live_block_rows, gated, sq, flat, output_weight, heads, positions)
    return mixed.reshape(hidden.shape), new_state


def solution(mesh):
    in_specs = (
        P(("rep", "row"), None, "head"),
        P("head"),
        P("row", "head"),
        P("row", "head"),
        P("row", "head"),
        P("row", None),
        P("head"),
        P("head"),
        P("head"),
        P("head"),
        P("row", "head", None),
        P("row", None, "head"),
        P("head", None),
        P(("rep", "row"), "head", None, None),
        P(("rep", "row")),
        P(("rep", "row")),
    )
    out_specs = (P(("rep", "row"), None, "head"), P(("rep", "row"), "head", None, None))
    return jax.shard_map(
        functools.partial(on_device, mesh.shape["head"], mesh.shape["row"]),
        mesh=mesh, in_specs=in_specs, out_specs=out_specs, check_vma=False,
    )
```

```python
import functools

import jax
import jax.numpy as jnp
from jax import lax
from jax.experimental import pallas as pl
from jax.experimental.pallas import tpu as pltpu
from jax.sharding import PartitionSpec as P

EPSILON = 1e-05
GROUP = 4
BF16 = jnp.bfloat16
F32 = jnp.float32
MESH = pl.DeviceIdType.MESH
LIMIT = 48 * 1024 * 1024
ANY = pl.BlockSpec(memory_space=pl.ANY)
VM = pl.BlockSpec(memory_space=pltpu.VMEM)
SM = pl.BlockSpec(memory_space=pltpu.SMEM)


def nt(a, b):
    return lax.dot_general(a, b, (((1,), (1,)), ((), ())), preferred_element_type=F32)


def split2(a):
    high = a.astype(BF16)
    return high, (a - high.astype(F32)).astype(BF16)


def front_kernel(
    capacity, positions, index_ref, hidden_ref, scale_ref, down_ref, scaled_ref, stats_ref,
    dbuf, sems,
):
    tokens = hidden_ref.shape[0]
    rank = down_ref.shape[1]
    copies = []
    for s in range(tokens // positions):
        copy = pltpu.make_async_copy(
            down_ref.at[lax.rem(index_ref[s], capacity)],
            dbuf.at[s * rank : (s + 1) * rank, :], sems.at[s],
        )
        copy.start()
        copies.append(copy)
    wide = hidden_ref[...].astype(F32)
    scaled_ref[...] = (wide * scale_ref[...]).astype(BF16)
    squares = jnp.sum(wide * wide, -1, keepdims=True)
    streams = 2 * GROUP
    rows = streams * positions
    lanes = streams * rank
    row = lax.broadcasted_iota(jnp.int32, (rows, lanes), 0) // positions
    col = lax.broadcasted_iota(jnp.int32, (rows, lanes), 1) // rank
    for g in range(tokens // rows):
        for copy in copies[g * streams : (g + 1) * streams]:
            copy.wait()
        here = slice(g * rows, (g + 1) * rows)
        low = nt(scaled_ref[here, :], dbuf[g * lanes : (g + 1) * lanes, :])
        low = jnp.where(row < GROUP, low, pltpu.roll(low, lanes // 2, 1))
        low = jnp.where(lax.rem(row, GROUP) == col, low, 0.0)
        stats_ref[here, :] = jnp.where(col < GROUP, low, squares[here, :])


def front(hidden, scale, down, index, positions):
    tokens, width = hidden.shape
    capacity, rank, _ = down.shape
    streams = tokens // positions
    return pl.pallas_call(
        functools.partial(front_kernel, capacity, positions),
        in_specs=[SM, VM, VM, ANY],
        out_specs=[VM, VM],
        out_shape=[
            jax.ShapeDtypeStruct((tokens, width), BF16),
            jax.ShapeDtypeStruct((tokens, 128), F32),
        ],
        scratch_shapes=[
            pltpu.VMEM((streams * rank, width), BF16),
            pltpu.SemaphoreType.DMA((streams,)),
        ],
        compiler_params=pltpu.CompilerParams(vmem_limit_bytes=57 * 1024 * 1024),
        name="front",
    )(index, hidden, scale.reshape(1, -1), down)


def project_kernel(
    heads, rows, model_width, scaled_ref, stats_ref, wsig_ref, wgate_ref, wstep_ref, wbc_ref,
    proj_ref, low_ref,
    wsig, wgate, wstep, wbc, xbuf, pbuf, rup, rdown, sbuf,
    w_sem, send_a, recv_a, send_b, recv_b, send_f, recv_f, send_s, recv_s, send_r, recv_u, recv_d,
):
    h = lax.axis_index("head")
    r = lax.axis_index("row")
    tokens, width = scaled_ref.shape
    share = heads // rows
    pieces = min(heads, tokens // 16)
    every = heads // pieces
    prow = tokens // pieces
    inner = wsig.shape[1]
    heads_here = wstep.shape[0]
    loads = [
        pltpu.make_async_copy(s, d, w_sem.at[i])
        for i, (s, d) in enumerate(
            [(wbc_ref, wbc), (wstep_ref, wstep), (wsig_ref, wsig), (wgate_ref, wgate)]
        )
    ]
    for load in loads:
        load.start()
    target_row = h // share
    piece = h // every

    def when(condition):
        return (lambda f: f()) if condition is True else pl.when(condition)

    is_owner = True if every == 1 else (lax.rem(h, every) == 0)

    barrier = pltpu.get_barrier_semaphore()
    for d in range(1, heads):
        pl.semaphore_signal(
            barrier, inc=1, device_id={"head": lax.rem(h + d, heads)}, device_id_type=MESH
        )
    for d in range(1, rows):
        pl.semaphore_signal(
            barrier, inc=1, device_id={"row": lax.rem(r + d, rows)}, device_id_type=MESH
        )

    @when(is_owner)
    def _():
        for j in range(share):
            for e in range(rows):
                src_h = r * share + j
                src_r = lax.rem(r + e, rows)
                same = jnp.logical_and(src_h == h, src_r == r)

                @pl.when(jnp.logical_not(same))
                def _():
                    pl.semaphore_signal(
                        barrier, inc=1, device_id={"head": src_h, "row": src_r},
                        device_id_type=MESH,
                    )

    to_self = jnp.logical_and(lax.rem(h, every) == 0, target_row == r).astype(jnp.int32)
    pl.semaphore_wait(barrier, heads - 1 + rows - 1 + pieces - to_self)

    def a_parts(k):
        src = scaled_ref.at[pl.ds(k * prow, prow), :]
        row0 = pl.multiple_of(r * tokens + k * prow, 16)
        col0 = pl.multiple_of(lax.rem(h, share) * width, 128)
        return src, xbuf.at[pl.ds(row0, prow), pl.ds(col0, width)]

    def a_remote(k):
        src, dst = a_parts(k)
        return pltpu.make_async_remote_copy(
            src_ref=src, dst_ref=dst, send_sem=send_a.at[k],
            recv_sem=recv_a.at[r * share + lax.rem(h, share)],
            device_id={"head": k * every, "row": target_row}, device_id_type=MESH,
        )

    def a_same(k):
        return jnp.logical_and(h == k * every, target_row == r)

    for k in range(pieces):
        @pl.when(jnp.logical_not(a_same(k)))
        def _():
            a_remote(k).start()

        @pl.when(a_same(k))
        def _():
            src, dst = a_parts(k)
            pltpu.make_async_copy(src, dst, recv_a.at[r * share + lax.rem(h, share)]).start()

    stat_copies = []
    for d in range(1, heads):
        copy = pltpu.make_async_remote_copy(
            src_ref=stats_ref, dst_ref=sbuf.at[d], send_sem=send_s.at[d], recv_sem=recv_s.at[d],
            device_id={"head": lax.rem(h + d, heads)}, device_id_type=MESH,
        )
        copy.start()
        stat_copies.append(copy)

    pbuf[:, 2 * inner + wbc.shape[1] :] = jnp.zeros((rows * tokens, 128), BF16)

    def block_rows(e, k):
        row0 = lax.rem(r + e, rows) * tokens + k * prow
        return xbuf.at[pl.ds(pl.multiple_of(row0, 16), prow), :]

    chips = heads // 2
    chip, core = h // 2, lax.rem(h, 2)
    partner = chip * 2 + 1 - core

    def owns(head):
        return True if every == 1 else lax.rem(head, every) == 0

    def b_copy(dx, e, k):
        to = lax.rem(chip + dx, chips) * 2 + core if dx else partner
        return pltpu.make_async_remote_copy(
            src_ref=block_rows(e, k), dst_ref=block_rows(e, k),
            send_sem=send_b.at[dx, e], recv_sem=recv_b.at[dx, e],
            device_id={"head": to}, device_id_type=MESH,
        )

    def origin(dx, its_core):
        return lax.rem(chip - dx + chips, chips) * 2 + its_core

    def f_copy(dx, e, its_core):
        block = block_rows(e, origin(dx, its_core) // every)
        return pltpu.make_async_remote_copy(
            src_ref=block, dst_ref=block,
            send_sem=send_f.at[dx, e], recv_sem=recv_f.at[dx, e],
            device_id={"head": partner}, device_id_type=MESH,
        )

    @when(is_owner)
    def _():
        for e in range(rows):
            src_r = lax.rem(r + e, rows)
            for j in range(share):
                dst = xbuf.at[
                    pl.ds(pl.multiple_of(src_r * tokens + piece * prow, 16), prow),
                    pl.ds(j * width, width),
                ]
                pltpu.make_async_copy(dst, dst, recv_a.at[src_r * share + j]).wait()
            for dx in list(range(1, chips)) + [0]:
                b_copy(dx, e, piece).start()

    for e in range(rows):
        for dx in range(1, chips):
            @when(owns(origin(dx, core)))
            def _():
                b_copy(dx, e, origin(dx, core) // every).wait_recv()
                f_copy(dx, e, core).start()

    for e in range(rows):
        @when(owns(partner))
        def _():
            b_copy(0, e, partner // every).wait_recv()

        for dx in range(1, chips):
            @when(owns(origin(dx, 1 - core)))
            def _():
                f_copy(dx, e, 1 - core).wait_recv()

    bc_width = wbc.shape[1]
    half = min(inner, 256)
    chunks = [(wbc, 0, bc_width, 2 * inner, 0), (wstep, None, 128, 2 * inner + bc_width, 1)]
    for i, w in ((2, wsig), (3, wgate)):
        for c in range(0, inner, half):
            chunks.append((w, c, half, (i - 2) * inner + c, i))

    def columns(n):
        return slice(chunks[n][3], chunks[n][3] + chunks[n][2])

    def hop(t, n, up):
        there = lax.rem(r + (1 if up else rows - 1), rows)
        return pltpu.make_async_remote_copy(
            src_ref=pbuf.at[t * tokens : (t + 1) * tokens, columns(n)],
            dst_ref=(rup if up else rdown).at[t, :, columns(n)],
            send_sem=send_r.at[t, n], recv_sem=(recv_u if up else recv_d).at[t, n],
            device_id={"row": there}, device_id_type=MESH,
        )

    def first_hop(n):
        @pl.when(r == 0)
        def _():
            for t in range(rows - 1, 0, -1):
                hop(t, n, True).start()

        @pl.when(r == rows - 1)
        def _():
            for t in range(rows - 1):
                hop(t, n, False).start()

    def pass_on(t, n, up):
        copy = hop(t, n, up)
        copy.wait_recv()
        here = slice(t * tokens, (t + 1) * tokens)
        came = (rup if up else rdown)[t, :, columns(n)]
        pbuf[here, columns(n)] = (
            pbuf[here, columns(n)].astype(F32) + came.astype(F32)
        ).astype(BF16)
        copy.start()

    waited = set()
    for n, (w, c, cw, out, load) in enumerate(chunks):
        if load not in waited:
            loads[load].wait()
            waited.add(load)
        if c is None:
            pbuf[:, out : out + heads_here] = nt(xbuf[...], w[...]).astype(BF16)
        else:
            pbuf[:, out : out + cw] = jnp.dot(
                xbuf[...], w[:, c : c + cw], preferred_element_type=F32
            ).astype(BF16)
        first_hop(n)

    for step in range(len(chunks) + rows - 3):
        for k in range(1, rows - 1):
            n = step - (k - 1)
            if 0 <= n < len(chunks):
                @pl.when(r == k)
                def _():
                    for t in range(rows - 1, k, -1):
                        pass_on(t, n, True)

                @pl.when(r == rows - 1 - k)
                def _():
                    for t in range(rows - 1 - k):
                        pass_on(t, n, False)

    total = stats_ref[...]
    for d in range(1, heads):
        stat_copies[d - 1].wait_recv()
        total = total + sbuf[d]
    inverse = lax.rsqrt(total[:, 127:128] / model_width + EPSILON)
    low_ref[...] = total * inverse
    own = pl.ds(pl.multiple_of(r * tokens, 16), tokens)
    for n in range(len(chunks)):
        proj_ref[:, columns(n)] = pbuf[own, columns(n)].astype(F32)
        for buffer, sem, there in ((rup, recv_u, r > 0), (rdown, recv_d, r < rows - 1)):
            @pl.when(there)
            def _():
                came = buffer.at[r, :, columns(n)]
                pltpu.make_async_copy(came, came, sem.at[r, n]).wait()
                proj_ref[:, columns(n)] = proj_ref[:, columns(n)] + came[...].astype(F32)
        proj_ref[:, columns(n)] = proj_ref[:, columns(n)] * inverse

    for n in range(len(chunks)):
        for t in range(rows):
            @pl.when(t > r)
            def _():
                hop(t, n, True).wait_send()

            @pl.when(t < r)
            def _():
                hop(t, n, False).wait_send()
    for copy in stat_copies:
        copy.wait_send()
    for k in range(pieces):
        @pl.when(jnp.logical_not(a_same(k)))
        def _():
            a_remote(k).wait_send()

    @when(is_owner)
    def _():
        for e in range(rows):
            for dx in range(chips):
                b_copy(dx, e, piece).wait_send()

    for e in range(rows):
        for dx in range(1, chips):
            @when(owns(origin(dx, core)))
            def _():
                f_copy(dx, e, core).wait_send()


def project(scaled, stats, wsig, wgate, wstep, wbc, heads, rows):
    tokens, width = scaled.shape
    depth, inner = wsig.shape
    out_width = 2 * inner + wbc.shape[1] + 128
    share = heads // rows
    pieces = min(heads, tokens // 16)
    n_chunks = 2 + 2 * (inner // min(inner, 256))
    dma = pltpu.SemaphoreType.DMA
    return pl.pallas_call(
        functools.partial(project_kernel, heads, rows, float(width * heads)),
        out_shape=[
            jax.ShapeDtypeStruct((tokens, out_width), F32),
            jax.ShapeDtypeStruct((tokens, 128), F32),
        ],
        in_specs=[VM, VM, ANY, ANY, ANY, ANY],
        out_specs=[VM, VM],
        scratch_shapes=[
            pltpu.VMEM(wsig.shape, BF16),
            pltpu.VMEM(wgate.shape, BF16),
            pltpu.VMEM(wstep.shape, BF16),
            pltpu.VMEM(wbc.shape, BF16),
            pltpu.VMEM((rows * tokens, depth), BF16),
            pltpu.VMEM((rows * tokens, out_width), BF16),
            pltpu.VMEM((rows, tokens, out_width), BF16),
            pltpu.VMEM((rows, tokens, out_width), BF16),
            pltpu.VMEM((heads, tokens, 128), F32),
            dma((4,)),
            dma((pieces,)),
            dma((rows * share,)),
            dma((heads // 2, rows)),
            dma((heads // 2, rows)),
            dma((heads // 2, rows)),
            dma((heads // 2, rows)),
            dma((heads,)),
            dma((heads,)),
            dma((rows, n_chunks)),
            dma((rows, n_chunks)),
            dma((rows, n_chunks)),
        ],
        compiler_params=pltpu.CompilerParams(
            collective_id=0, has_side_effects=True, vmem_limit_bytes=LIMIT
        ),
        name="project",
    )(scaled, stats, wsig, wgate, wstep, wbc)


def scan_kernel(
    positions, index_ref, live_ref, proj_ref, low_ref, bias_ref, rate_ref, skip_ref, gain_ref,
    spread_ref, state_ref, *rest
):
    ups, (new_ref, gated_ref, sq_ref) = rest[:GROUP], rest[GROUP:]
    g = pl.program_id(0)
    rows = proj_ref.shape[0]
    inner = ups[0].shape[2]
    rank = ups[0].shape[1]
    n_state = state_ref.shape[3]
    shape_state = state_ref.shape[1:]
    base = 2 * inner
    xin = proj_ref[:, :inner]
    zin = proj_ref[:, inner:base]
    bc = proj_ref[:, base : base + 2 * n_state]
    dtin = proj_ref[:, base + 2 * n_state :]
    low = low_ref[:, : GROUP * rank].astype(BF16)
    up = jnp.concatenate([u[0] for u in ups], axis=0)
    x = jax.nn.silu(xin + jnp.dot(low, up, preferred_element_type=F32))
    bgate = jax.nn.silu(bc[:, :n_state])
    cgate = jax.nn.silu(bc[:, n_state:])
    row1 = lax.broadcasted_iota(jnp.int32, (rows, 1), 0)
    stream1 = row1 // positions
    live = (g * GROUP + stream1) < live_ref[0]

    def padded(ref):
        blank = jnp.zeros((1, dtin.shape[1] - ref.shape[1]), F32)
        return jnp.concatenate([ref[...], blank], axis=1)

    dt = jax.nn.softplus(dtin + padded(bias_ref))
    decay = jnp.exp(-dt * padded(rate_ref))
    sk_high, sk_low = split2(jnp.broadcast_to(padded(skip_ref), dt.shape))
    dt_high, dt_low = split2(dt)
    de_high, de_low = split2(decay)
    spread = jnp.dot(
        jnp.concatenate([dt_high, dt_low, de_high, de_low, sk_high, sk_low], axis=0), spread_ref[...],
        preferred_element_type=F32,
    )
    dt_wide = spread[:rows] + spread[rows : 2 * rows]
    de_wide = spread[2 * rows : 3 * rows] + spread[3 * rows : 4 * rows]
    u = jnp.where(live, dt_wide * x, 0.0)
    de_wide = jnp.where(live, de_wide, 1.0)

    second = lax.rem(row1, positions) == 1
    prev_de = pltpu.roll(de_wide, 1, 0)
    prev_u = pltpu.roll(u, 1, 0)
    prev_b = pltpu.roll(bgate, 1, 0)
    keep = jnp.where(second, de_wide * prev_de, de_wide)
    carried_u = jnp.where(second, u, u * pltpu.roll(de_wide, rows - 1, 0))
    keep_high, keep_low = split2(keep)
    left = jnp.concatenate(
        [carried_u.astype(BF16), keep_high, keep_low, jnp.zeros_like(keep_low)], axis=0
    )
    left = left.T
    y = jnp.zeros((rows, inner), F32)
    zero_b = jnp.zeros((rows, n_state), F32)
    for j in range(GROUP):
        mine = stream1 == j
        b_mine = jnp.where(mine, bgate, 0.0)
        ones_mine = jnp.broadcast_to(jnp.where(mine & second, 1.0, 0.0), (rows, n_state))
        right = jnp.concatenate(
            [
                jnp.concatenate([b_mine, zero_b], axis=1),
                jnp.concatenate([zero_b, ones_mine], axis=1),
                jnp.concatenate([zero_b, ones_mine], axis=1),
                jnp.concatenate([zero_b, zero_b], axis=1),
            ],
            axis=0,
        ).astype(BF16)
        state = state_ref[j].reshape(inner, n_state)
        both = jnp.dot(left, right, preferred_element_type=F32)
        new = state.astype(F32) * both[:, n_state:] + both[:, :n_state]
        new_ref[j] = new.astype(BF16).reshape(shape_state)
        y = y + nt(jnp.where(mine, cgate, 0.0).astype(BF16), state)

    dot_own = jnp.sum(bgate * cgate, -1, keepdims=True)
    dot_prev = jnp.sum(prev_b * cgate, -1, keepdims=True)
    y = keep * y + u * dot_own + jnp.where(second, de_wide * prev_u * dot_prev, 0.0)
    y = y + (spread[4 * rows : 5 * rows] + spread[5 * rows :]) * x
    gated = y * jax.nn.silu(zin)
    gated_ref[...] = (gated * gain_ref[...]).astype(BF16)
    sq_ref[...] = jnp.broadcast_to(jnp.sum(gated * gated, -1, keepdims=True), sq_ref.shape)


def scan(index, live, proj, low, bias, rate, skip, gain, state, up, positions):
    tokens, out_width = proj.shape
    capacity, rank, inner = up.shape
    rows = GROUP * positions
    heads_here = bias.shape[0]
    head_size = inner // heads_here
    spread = (jnp.arange(128)[:, None] == jnp.arange(inner)[None, :] // head_size).astype(BF16)
    bias, rate, skip = bias.reshape(1, -1), rate.reshape(1, -1), skip.reshape(1, -1)

    def up_spec(j):
        return pl.BlockSpec(
            (1, rank, inner), lambda g, idx, lv: (lax.rem(idx[g * GROUP + j], capacity), 0, 0)
        )

    def whole(a):
        return pl.BlockSpec(a.shape, lambda g, idx, lv: (0, 0))

    def by_rows(w):
        return pl.BlockSpec((rows, w), lambda g, idx, lv: (g, 0))

    gain = gain.reshape(1, -1)
    state_spec = pl.BlockSpec((GROUP,) + state.shape[1:], lambda g, idx, lv: (g, 0, 0, 0))
    return pl.pallas_call(
        functools.partial(scan_kernel, positions),
        grid_spec=pltpu.PrefetchScalarGridSpec(
            num_scalar_prefetch=2,
            grid=(tokens // rows,),
            in_specs=[by_rows(out_width), by_rows(128), whole(bias), whole(rate), whole(skip),
                      whole(gain), whole(spread), state_spec]
            + [up_spec(j) for j in range(GROUP)],
            out_specs=[state_spec, by_rows(inner), by_rows(128)],
        ),
        out_shape=[
            jax.ShapeDtypeStruct(state.shape, BF16),
            jax.ShapeDtypeStruct((tokens, inner), BF16),
            jax.ShapeDtypeStruct((tokens, 128), F32),
        ],
        compiler_params=pltpu.CompilerParams(vmem_limit_bytes=LIMIT),
        name="scan",
    )(index, live, proj, low, bias, rate, skip, gain, spread, state, *([up] * GROUP))


def output_kernel(
    heads, positions, inner_width, live_ref, gated_ref, sq_ref, hidden_ref, w_ref, out_ref,
    wbuf, pbuf, rbuf, sbuf, w_sem, send_s, recv_s, send_r, recv_r,
):
    h = lax.axis_index("head")
    tokens, width = hidden_ref.shape
    chips = heads // 2
    chip, core = h // 2, lax.rem(h, 2)
    partner = chip * 2 + 1 - core
    order = [2 * dx + k for dx in list(range(1, chips)) + [0] for k in range(2)]

    def target(d):
        its_core = core if d % 2 else 1 - core
        return lax.rem(chip + d // 2, chips) * 2 + its_core

    def load(d):
        to = target(d)
        return pltpu.make_async_copy(
            w_ref.at[:, pl.ds(pl.multiple_of(to * width, 128), width)], wbuf.at[d], w_sem.at[d]
        )

    for d in order:
        load(d).start()
    barrier = pltpu.get_barrier_semaphore()
    for d in range(1, heads):
        pl.semaphore_signal(
            barrier, inc=1, device_id={"head": lax.rem(h + d, heads)}, device_id_type=MESH
        )
    pl.semaphore_wait(barrier, heads - 1)
    copies = []
    for d in range(1, heads):
        copy = pltpu.make_async_remote_copy(
            src_ref=sq_ref, dst_ref=sbuf.at[d], send_sem=send_s.at[d], recv_sem=recv_s.at[d],
            device_id={"head": lax.rem(h + d, heads)}, device_id_type=MESH,
        )
        copy.start()
        copies.append(copy)
    parts = {}
    step = min(width, 512)
    for d in order:
        load(d).wait()
        for c in range(0, width, step):
            pbuf[d, :, c : c + step] = jnp.dot(
                gated_ref[...], wbuf[d, :, c : c + step], preferred_element_type=F32
            ).astype(BF16)
        if d == 1:
            continue
        if d % 2:
            parts[d - 1].wait_recv()
            pbuf[d] = (pbuf[d].astype(F32) + rbuf[d - 1].astype(F32)).astype(BF16)
        copy = pltpu.make_async_remote_copy(
            src_ref=pbuf.at[d], dst_ref=rbuf.at[d], send_sem=send_r.at[d],
            recv_sem=recv_r.at[d],
            device_id={"head": target(d) if d % 2 else partner}, device_id_type=MESH,
        )
        copy.start()
        parts[d] = copy
    square = sq_ref[...]
    for d in range(1, heads):
        copies[d - 1].wait_recv()
        square = square + sbuf[d]
    inverse = lax.rsqrt(square[:, :1] / inner_width + EPSILON)
    mixer = pbuf[1].astype(F32)
    for d in [0] + [2 * dx + 1 for dx in range(1, chips)]:
        parts[d].wait_recv()
        mixer = mixer + rbuf[d].astype(F32)
    stream = lax.broadcasted_iota(jnp.int32, (tokens, 1), 0) // positions
    live = stream < live_ref[0]
    out_ref[...] = (
        hidden_ref[...].astype(F32) + jnp.where(live, mixer * inverse, 0.0)
    ).astype(BF16)
    for copy in copies:
        copy.wait_send()
    for copy in parts.values():
        copy.wait_send()


def output(live, gated, sq, hidden, weight, heads, positions):
    tokens, width = hidden.shape
    inner = gated.shape[1]
    dma = pltpu.SemaphoreType.DMA
    return pl.pallas_call(
        functools.partial(output_kernel, heads, positions, float(inner * heads)),
        out_shape=jax.ShapeDtypeStruct((tokens, width), BF16),
        in_specs=[SM, VM, VM, VM, ANY],
        out_specs=VM,
        scratch_shapes=[
            pltpu.VMEM((heads, inner, width), BF16),
            pltpu.VMEM((heads, tokens, width), BF16),
            pltpu.VMEM((heads, tokens, width), BF16),
            pltpu.VMEM((heads, tokens, 128), F32),
            dma((heads,)),
            dma((heads,)),
            dma((heads,)),
            dma((heads,)),
            dma((heads,)),
        ],
        compiler_params=pltpu.CompilerParams(
            collective_id=1, has_side_effects=True, vmem_limit_bytes=LIMIT
        ),
        name="output",
    )(live, gated, sq, hidden, weight)


def on_device(
    heads, rows,
    hidden, input_norm_scale, projection_signal, projection_gate, projection_step,
    projection_input_output, step_bias, head_decay_rate, head_skip_weight, gated_norm_scale,
    adapter_down_weight, adapter_up_weight, output_weight, scan_state, stream_tenant_index,
    live_block_rows,
):
    streams, positions, width = hidden.shape
    flat = hidden.reshape(streams * positions, width)
    down = jnp.swapaxes(adapter_down_weight, 1, 2)
    scaled, stats = front(flat, input_norm_scale, down, stream_tenant_index, positions)
    proj, low = project(
        scaled, stats, projection_signal, projection_gate, projection_step.T,
        projection_input_output, heads, rows,
    )
    new_state, gated, sq = scan(
        stream_tenant_index, live_block_rows, proj, low, step_bias, head_decay_rate,
        head_skip_weight, gated_norm_scale, scan_state, adapter_up_weight, positions,
    )
    mixed = output(live_block_rows, gated, sq, flat, output_weight, heads, positions)
    return mixed.reshape(hidden.shape), new_state


def solution(mesh):
    in_specs = (
        P(("rep", "row"), None, "head"),
        P("head"),
        P("row", "head"),
        P("row", "head"),
        P("row", "head"),
        P("row", None),
        P("head"),
        P("head"),
        P("head"),
        P("head"),
        P("row", "head", None),
        P("row", None, "head"),
        P("head", None),
        P(("rep", "row"), "head", None, None),
        P(("rep", "row")),
        P(("rep", "row")),
    )
    out_specs = (P(("rep", "row"), None, "head"), P(("rep", "row"), "head", None, None))
    return jax.shard_map(
        functools.partial(on_device, mesh.shape["head"], mesh.shape["row"]),
        mesh=mesh, in_specs=in_specs, out_specs=out_specs, check_vma=False,
    )
```
